256 devices in a mesh: seq: 32 (over y, z_lo, core), exp: 8 (over z_hi, x).
Axes of the slice: x: 4, y: 4, z: 8 (z_hi: 2, z_lo: 4; z = z_hi * 4 + z_lo), core: 2. Of those that a mesh axis runs over, the one named last changes fastest.
Arguments:
- hidden_in: bfloat16 [24, 6144], P('exp', 'seq'), may hold values from -2 to 2
- queries: bfloat16 [24, 6144], P(None, 'exp'), may hold values from -40 to 40
- key_cache: bfloat16 [24, 8192, 1024], P(None, 'seq', 'exp'), may hold values from -16 to 16
- value_cache: bfloat16 [24, 8192, 1024], P(None, 'seq', 'exp'), may hold values from -6 to 6
- lengths: int32 [24], replicated, may hold values from 2 to 8192
- out_weight: bfloat16 [6144, 6144], P('exp', 'seq'), may hold values from -0.078125 to 0.078125
- norm_gain: float32 [6144], P('seq'), may hold values from 0.1 to 1.9
- router: bfloat16 [6144, 8], P('seq'), may hold values from -0.078125 to 0.078125
- expert_ids: int32 [24, 2], P('exp'), may hold values from 0 to 7, as said below
- capacity: int32 [8], replicated, may hold values from 1 to 3, as said below
- w_gate: bfloat16 [8, 6144, 8192], P('exp', None, 'seq'), may hold values from -0.078125 to 0.078125
- w_up: bfloat16 [8, 6144, 8192], P('exp', None, 'seq'), may hold values from -0.078125 to 0.078125
- w_down: bfloat16 [8, 8192, 6144], P('exp', 'seq'), may hold values from -0.125 to 0.125
Outputs:
- layer_out: bfloat16 [24, 6144], P('exp', 'seq')
The draws below stay inside these ranges and needn't reach their ends.
Inputs may be any that keep to these rules, and one draw needn't show every extreme that they name: lengths[b] counts sequence b's live cache positions, the newest token's included. `expert_ids`: the two experts of a token differ. One expert is named by every token; any other expert is named at most 3 times within one aligned block of 3 tokens. The expert that every token names has capacity 3.
All inputs are finite; a program needn't handle non-finite values.
Results may differ from the reference program's by a relative error of at most 0.0085.
Values may be sent and summed in bfloat16 or wider, within the bound.
No kernel may reach another device: no remote copies, remote signals or barrier semaphores. Data moves between devices by JAX's collectives and lax.ppermute only.
A program may use at most 64 MiB of HBM per device.

```python
import math
import jax
import jax.numpy as jnp
from jax import lax

D = 6144
HEADS = 48
KV_HEADS = 8
HEAD_DIM = 128
EXPERTS = 8
FF_W = 8192
TOK_DEV = 3
LENGTH = 8192
SEQS = 24


def hot_expert(key):
    return jax.random.randint(jax.random.fold_in(key, 11), (), 0, EXPERTS)


def draw_expert_ids(key, part):
    favored = hot_expert(key)
    offsets = jax.random.randint(jax.random.fold_in(key, 12), (SEQS,), 1, EXPERTS)
    other_ids = (favored + offsets) % EXPERTS
    flipped = jax.random.randint(jax.random.fold_in(key, 13), (SEQS,), 0, 2)
    first_ids = jnp.where(flipped == 1, other_ids, favored)
    second_ids = jnp.where(flipped == 1, favored, other_ids)
    return jnp.stack([first_ids, second_ids], axis=1).astype(jnp.int32)


def draw_capacity(key, part):
    favored = hot_expert(key)
    limits = jax.random.randint(jax.random.fold_in(key, 14), (EXPERTS,), 1, TOK_DEV + 1)
    return jnp.where(jnp.arange(EXPERTS) == favored, TOK_DEV, limits).astype(jnp.int32)


def draw_queries(key, part):
    return jnp.clip(2.5 * jax.random.normal(jax.random.fold_in(key, 32), (SEQS, HEADS * HEAD_DIM), jnp.float32), -15.0, 15.0).astype(jnp.bfloat16)


def draw_key_cache(key, part):
    key_rows = jnp.clip(jax.random.normal(jax.random.fold_in(key, 33), (SEQS, LENGTH, KV_HEADS * HEAD_DIM), jnp.float32), -6.0, 6.0)
    return key_rows.astype(jnp.bfloat16)


def touch_ends(values, rng, least, largest):
    extent = values.shape
    place = [jax.random.randint(jax.random.fold_in(rng, axis), (), 0, extent[axis]) for axis in range(len(extent))]
    values = values.at[tuple(place)].set(least)
    longest = extent.index(max(extent))
    place[longest] = (place[longest] + 1) % extent[longest]
    return values.at[tuple(place)].set(largest)


def spiked(result, stream_key, source, target, parts, factor):
    def block_of(axis_at):
        return (jnp.arange(result.shape[axis_at]) // (result.shape[axis_at] // parts)).reshape((-1,) + (1,) * (result.ndim - 1 - axis_at))

    near = jax.random.permutation(stream_key, parts)[block_of(target)]
    second = (block_of(target) + parts // 2) % parts
    return jnp.where((block_of(source) == near) | (block_of(source) == second), factor * result, result)


def level_of(own_key, shape, split, smallest, largest):
    level = 1.0
    for axis_at, shards_of in split:
        draws = jax.random.uniform(jax.random.fold_in(jax.random.fold_in(own_key, 6), axis_at), (shards_of,), jnp.float32, smallest / len(split), largest / len(split))
        level = level * jnp.repeat(jnp.exp(draws), shape[axis_at] // shards_of).reshape((-1,) + (1,) * (len(shape) - 1 - axis_at))
    return level


def centred(own_key, dims, scale, most, shards=(), held_as=jnp.bfloat16):
    drawn = scale * jax.random.normal(own_key, dims, jnp.float32)
    if shards:
        drawn = drawn * level_of(own_key, dims, shards, -0.22, 0.18)
    return jnp.clip(drawn, -most, most).astype(held_as)


def heavy_noise(own_key, extent, width, limit, shards, heavy, kind=jnp.bfloat16):
    array = width * jax.random.normal(own_key, extent, jnp.float32)
    if shards:
        array = array * level_of(own_key, extent, shards, -0.22, 0.18)
    return jnp.clip(spiked(array, jax.random.fold_in(own_key, 3), *heavy), -limit, limit).astype(kind)


def setup_inputs(seed: int = 0) -> dict:
    arg_keys = jax.random.split(jax.random.key(seed), 14)
    return {
        "hidden_in": centred(arg_keys[0], (SEQS, D), 0.3, 2.0, ((0, 8), (1, 32))),
        "queries": draw_queries(jax.random.fold_in(arg_keys[13], 71), 0),
        "key_cache": draw_key_cache(jax.random.fold_in(arg_keys[13], 71), 0),
        "value_cache": centred(arg_keys[3], (SEQS, LENGTH, KV_HEADS * HEAD_DIM), 1.0, 6.0, ((1, 32), (2, 8))),
        "lengths": touch_ends(jax.random.randint(arg_keys[4], (SEQS,), 2, LENGTH + 1), jax.random.fold_in(arg_keys[4], 1), 2, LENGTH).astype(jnp.int32),
        "out_weight": centred(arg_keys[5], (HEADS * HEAD_DIM, D), (HEADS * HEAD_DIM) ** -0.5, 0.078125, ((0, 8), (1, 32))),
        "norm_gain": jnp.clip(1.0 + 0.18 * jax.random.normal(arg_keys[6], (D,), jnp.float32), 0.1, 1.9),
        "router": centred(arg_keys[7], (D, EXPERTS), D ** -0.5, 0.078125, ((0, 32),)),
        "expert_ids": draw_expert_ids(jax.random.fold_in(arg_keys[13], 71), 0),
        "capacity": draw_capacity(jax.random.fold_in(arg_keys[13], 71), 0),
        "w_gate": centred(arg_keys[10], (EXPERTS, D, FF_W), D ** -0.5, 0.078125, ((0, 8), (2, 32))),
        "w_up": centred(arg_keys[11], (EXPERTS, D, FF_W), D ** -0.5, 0.078125, ((0, 8), (2, 32))),
        "w_down": heavy_noise(arg_keys[12], (EXPERTS, FF_W, D), FF_W ** -0.5, 0.125, ((0, 8), (1, 32)), (1, 2, 32, 2.75)),
    }


masked_score = -1e+30
norm_eps = 1e-05

def expert_rows(normed, gate_mat, up_mat, down_weight_matrix):
    gate_sum = jnp.dot(normed, gate_mat, preferred_element_type=jnp.float32)
    up_sum = jnp.dot(normed, up_mat, preferred_element_type=jnp.float32)
    hidden_act = (jax.nn.silu(gate_sum) * up_sum).astype(jnp.bfloat16)
    return jnp.dot(hidden_act, down_weight_matrix, preferred_element_type=jnp.float32)

def reference(hidden_in, queries, key_cache, value_cache, lengths, out_weight, norm_gain, router, expert_ids, capacity, w_gate, w_up, w_down):
    group_size = HEADS // KV_HEADS
    query_heads = queries.astype(jnp.float32).reshape(SEQS, KV_HEADS, group_size, HEAD_DIM)
    positions = jnp.arange(LENGTH, dtype=jnp.int32)
    live_mask = positions[None, :] < lengths[:, None]
    outputs = []
    for kv_index in range(KV_HEADS):
        key_rows = key_cache[:, :, kv_index * HEAD_DIM:(kv_index + 1) * HEAD_DIM].astype(jnp.float32)
        value_rows = value_cache[:, :, kv_index * HEAD_DIM:(kv_index + 1) * HEAD_DIM].astype(jnp.float32)
        scores = jnp.einsum('bgd,bjd->bgj', query_heads[:, kv_index], key_rows, precision=lax.Precision.HIGHEST) * (1.0 / math.sqrt(HEAD_DIM))
        scores = jnp.where(live_mask[:, None, :], scores, masked_score)
        peak_score = lax.optimization_barrier(jnp.max(scores, axis=-1, keepdims=True))
        attn_weights = jnp.where(live_mask[:, None, :], jnp.exp(scores - peak_score), 0.0)
        denom_sum = lax.optimization_barrier(jnp.sum(attn_weights, axis=-1))
        weighted = jnp.einsum('bgj,bjd->bgd', attn_weights, value_rows, precision=lax.Precision.HIGHEST)
        outputs.append(weighted / denom_sum[..., None])
    attended = jnp.stack(outputs, axis=1).reshape(SEQS, HEADS * HEAD_DIM).astype(jnp.bfloat16)
    projected = jnp.dot(attended, out_weight, preferred_element_type=jnp.float32)
    residual = hidden_in.astype(jnp.float32) + projected
    scale_row = lax.rsqrt(lax.optimization_barrier(jnp.sum(residual * residual, axis=-1)) / D + norm_eps)
    gained = residual * norm_gain
    logits = jnp.dot(gained, router.astype(jnp.float32), precision=lax.Precision.HIGHEST) * scale_row[:, None]
    normed = (gained * scale_row[:, None]).astype(jnp.bfloat16)
    onehot_int = (expert_ids[:, :, None] == jnp.arange(EXPERTS, dtype=jnp.int32)[None, None, :]).astype(jnp.int32)
    name_count = lax.optimization_barrier(jnp.sum(onehot_int, axis=1))
    row_order = jnp.arange(SEQS, dtype=jnp.int32)
    row_block = row_order // TOK_DEV
    before = ((row_block[:, None] == row_block[None, :]) & (row_order[None, :] < row_order[:, None])).astype(jnp.int32)
    earlier = jnp.dot(before, name_count)
    slot_rank = lax.optimization_barrier(jnp.sum(onehot_int * earlier[:, None, :], axis=-1))
    slot_limit = lax.optimization_barrier(jnp.sum(onehot_int * capacity[None, None, :], axis=-1))
    kept_mask = (slot_rank < slot_limit).astype(jnp.float32)
    expert_indicator = onehot_int.astype(jnp.float32)
    chosen = lax.optimization_barrier(jnp.sum(expert_indicator * logits[:, None, :], axis=-1))
    gate_weight = jax.nn.sigmoid(chosen - chosen[:, ::-1])
    expert_output = lax.map(lambda mats: expert_rows(normed, mats[0], mats[1], mats[2]), (w_gate, w_up, w_down))
    selected_experts = jnp.einsum('hlw,whv->hlv', expert_indicator, expert_output, precision=lax.Precision.HIGHEST)
    combined = lax.optimization_barrier(jnp.sum((gate_weight * kept_mask)[:, :, None] * selected_experts, axis=1))
    return (residual + combined).astype(jnp.bfloat16)
```

```python
import functools
import math

import jax
import jax.numpy as jnp
from jax import lax
from jax.experimental import pallas as pl
from jax.experimental.pallas import tpu as pltpu
from jax.sharding import Mesh
from jax.sharding import PartitionSpec as P

D = 6144
HEADS = 48
KV_HEADS = 8
HEAD_DIM = 128
EXPERTS = 8
TOKENS = 24
OWNED = 3
GROUP = HEADS // KV_HEADS
COLS = 192
HALF = TOKENS // 2
SUB = 8
HALF_ROWS = HALF * SUB
CHIPS = 16
SEQ = ("seq_0", "seq_1", "seq_2")
masked_score = -1e30
norm_eps = 1e-05
f32 = jnp.float32
bf16 = jnp.bfloat16
VMEM = pl.BlockSpec(memory_space=pltpu.VMEM)
SMEM = pl.BlockSpec(memory_space=pltpu.SMEM)
ANY = pl.BlockSpec(memory_space=pl.ANY)


def lanes(shape):
    return lax.broadcasted_iota(jnp.int32, shape, len(shape) - 1)


def subs(shape):
    return lax.broadcasted_iota(jnp.int32, shape, len(shape) - 2)


def rounded(x):
    return x.astype(bf16).astype(f32)


CHUNKS = 4
PER = TOKENS // CHUNKS


def attention_kernel(where_ref, lengths_ref, q_ref, k_any, v_any, out_ref, kbuf, vbuf, qs, sems):
    copies = []
    for i in range(CHUNKS):
        part = pl.ds(i * PER, PER)
        copies.append(
            (
                pltpu.make_async_copy(k_any.at[part], kbuf.at[part], sems.at[0, i]),
                pltpu.make_async_copy(v_any.at[part], vbuf.at[part], sems.at[1, i]),
            )
        )
    for pair in copies:
        pair[0].start()
        pair[1].start()
    qs[...] = jnp.zeros_like(qs)
    for h in range(GROUP):
        qs[pl.ds(h, TOKENS, stride=SUB), :] = q_ref[:, h * HEAD_DIM : (h + 1) * HEAD_DIM].astype(f32)
    first = where_ref[0]
    span = k_any.shape[1]
    places = first + lanes((SUB, span))
    lane, sub = lanes((SUB, 128)), subs((SUB, 128))
    scale = 1.0 / math.sqrt(HEAD_DIM)
    for i in range(CHUNKS):
        copies[i][0].wait()
        scores = []
        for b in range(i * PER, (i + 1) * PER):
            query = qs[b * SUB : (b + 1) * SUB, :].astype(bf16)
            s = lax.dot_general(query, kbuf[b], (((1,), (1,)), ((), ())), preferred_element_type=f32)
            scores.append(jnp.where(places < lengths_ref[b], s * scale, masked_score))
        copies[i][1].wait()
        blocks = []
        for n, b in enumerate(range(i * PER, (i + 1) * PER)):
            s = scores[n]
            peak = rounded(jnp.max(s, axis=-1, keepdims=True))
            p = jnp.where(places < lengths_ref[b], jnp.exp(s - peak), 0.0)
            total = jnp.sum(p, axis=-1, keepdims=True)
            p_hi = rounded(p)
            both = jnp.concatenate([p_hi, p - p_hi], axis=0).astype(bf16)
            weighted = jnp.dot(both, vbuf[b], preferred_element_type=f32)
            weighted = weighted[:SUB] + weighted[SUB:]
            total_hi = rounded(total)
            stats = jnp.where(lane == sub, peak, 0.0)
            stats = jnp.where(lane == sub + SUB, total_hi, stats)
            stats = jnp.where(lane == sub + 2 * SUB, total - total_hi, stats)
            stats = jnp.sum(jnp.where(sub < GROUP, stats, 0.0), axis=0, keepdims=True)
            blocks.append(jnp.where(sub == GROUP, stats, weighted))
        for n in range(0, PER, 2):
            b = i * PER + n
            half, row = b // HALF, (b % HALF) * SUB
            two = jnp.concatenate([blocks[n], blocks[n + 1]], axis=0).astype(bf16)
            for y in range(4):
                out_ref[2 * y + half, row : row + 2 * SUB, :] = two


def combined(blocks):
    shape = (HALF, SUB, 128)
    lane, sub = lanes(shape), subs(shape)
    flat = lanes((HALF, 1, 128))
    stats = [jnp.sum(jnp.where(sub == GROUP, x, 0.0), axis=1, keepdims=True) for x in blocks]
    peak = functools.reduce(jnp.maximum, stats)
    factors = [jnp.exp(jnp.minimum(s - peak, 0.0)) for s in stats]
    total = jnp.zeros((HALF, 1, 128), f32)
    for s, factor in zip(stats, factors):
        total += factor * (pltpu.roll(s, 128 - SUB, 2) + pltpu.roll(s, 128 - 2 * SUB, 2))
    total = jnp.where(flat < GROUP, total, 1.0)
    return peak, factors, total


def as_column(x):
    shape = (HALF, SUB, 128)
    wide = jnp.broadcast_to(x, shape)
    return jnp.sum(jnp.where(lanes(shape) == subs(shape), wide, 0.0), axis=2, keepdims=True)


def merge_kernel(in_ref, out_ref):
    blocks = [in_ref[i].astype(f32).reshape(HALF, SUB, 128) for i in range(8)]
    peak, factors, total = combined(blocks)
    weighted = jnp.zeros((HALF, SUB, 128), f32)
    for x, factor in zip(blocks, factors):
        weighted += as_column(factor) * x
    flat = lanes((HALF, 1, 128))
    total_hi = rounded(total)
    stats = jnp.where(flat < SUB, peak, pltpu.roll(total_hi, SUB, 2))
    stats = jnp.where(flat < 2 * SUB, stats, pltpu.roll(total - total_hi, 2 * SUB, 2))
    stats = jnp.where(flat < 3 * SUB, stats, 0.0)
    sub = subs((HALF, SUB, 128))
    block = jnp.where(sub == GROUP, stats, weighted).reshape(HALF_ROWS, 128).astype(bf16)
    for i in range(8):
        out_ref[i] = block


def project_kernel(where_ref, ids_ref, in_ref, hidden_ref, weight_ref, out_ref, rest_ref, att, wide):
    for half in range(2):
        blocks = [in_ref[2 * z + half].astype(f32).reshape(HALF, SUB, 128) for z in range(4)]
        _, factors, total = combined(blocks)
        inverse = 1.0 / total
        weighted = jnp.zeros((HALF, SUB, 128), f32)
        for x, factor in zip(blocks, factors):
            weighted += as_column(factor * inverse) * x
        att[half * HALF_ROWS : (half + 1) * HALF_ROWS, :] = weighted.reshape(HALF_ROWS, 128)
    acc = jnp.zeros((TOKENS, COLS), f32)
    for h in range(GROUP):
        rows = att[pl.ds(h, TOKENS, stride=SUB), :].astype(bf16)
        acc += lax.dot_general(
            rows,
            weight_ref[:, h * HEAD_DIM : (h + 1) * HEAD_DIM],
            (((1,), (1,)), ((), ())),
            preferred_element_type=f32,
        )
    mine = OWNED * where_ref[1]
    row = subs((TOKENS, COLS))
    hidden = hidden_ref[...].astype(f32)
    for r in range(OWNED):
        acc += jnp.where(row == mine + r, hidden[r : r + 1, :], 0.0)
    tail = jnp.zeros((TOKENS, 64), f32)
    lane, row_tail = lanes((TOKENS, 64)), subs((TOKENS, 64))
    for r in range(OWNED):
        for k in range(2):
            here = (row_tail == mine + r) & (lane == k)
            tail = jnp.where(here, ids_ref[k, r].astype(f32), tail)
    wide[:, :COLS] = acc
    wide[:, COLS:] = tail
    full = wide[...]
    sent = full.astype(bf16)
    for i in range(8):
        out_ref[i] = sent
    row = subs((TOKENS, 256))
    owned = (row >= mine) & (row < mine + OWNED)
    rest_ref[...] = jnp.where(owned, full - sent.astype(f32), 0.0)


def gained_kernel(in_ref, rest_ref, gain_ref, router_ref, out_ref, residual_ref, wide):
    total = rest_ref[...]
    for i in range(8):
        total += in_ref[i].astype(f32)
    residual_ref[...] = total
    residual = total[:, :COLS]
    gained = residual * gain_ref[...]
    hi = gained.astype(bf16)
    lo = (gained - hi.astype(f32)).astype(bf16)
    over_features = (((1,), (1,)), ((), ()))
    logits = lax.dot_general(hi, router_ref[...], over_features, preferred_element_type=f32)
    logits += lax.dot_general(lo, router_ref[...], over_features, preferred_element_type=f32)
    squares = jnp.sum(residual * residual, axis=-1, keepdims=True)
    logits_hi, squares_hi = rounded(logits), rounded(squares)
    wide[...] = jnp.zeros_like(wide)
    wide[:, :COLS] = gained
    wide[:, COLS : COLS + 8] = logits_hi
    wide[:, COLS + 8 : COLS + 9] = squares_hi
    wide[:, COLS + 32 : COLS + 40] = logits - logits_hi
    wide[:, COLS + 40 : COLS + 41] = squares - squares_hi
    sent = wide[...].astype(bf16)
    for i in range(CHIPS):
        out_ref[i] = sent


def expert_kernel(
    where_ref, capacity_ref, own_ref, other_ref, residual_ref, gate_ref, up_ref, down_ref, keep_ref, send_ref
):
    core, me = where_ref[2], where_ref[1]
    stats = jnp.zeros((TOKENS, 128), f32)
    gate = jnp.zeros((TOKENS, 256), f32)
    up = jnp.zeros((TOKENS, 256), f32)
    for k in range(CHIPS):
        for ref, parity in ((own_ref, core), (other_ref, 1 - core)):
            stats += ref[k, :, 128:].astype(f32)
            rows = pl.ds(pl.multiple_of((2 * k + parity) * COLS, COLS), COLS)
            x = ref[k, :, :COLS]
            gate += jnp.dot(x, gate_ref[rows, :], preferred_element_type=f32)
            up += jnp.dot(x, up_ref[rows, :], preferred_element_type=f32)
    stats = pltpu.roll(stats, 64, 1) + pltpu.roll(stats, 32, 1)
    lane, row = lanes((TOKENS, 128)), subs((TOKENS, 128))

    def pick(x, place):
        return jnp.sum(jnp.where(lane == place, x, 0.0), axis=-1, keepdims=True)

    scale = lax.rsqrt(pick(stats, 8) / D + norm_eps)
    logits = stats * scale
    named = residual_ref[:, 128:]
    first, second = pick(named, 64).astype(jnp.int32), pick(named, 65).astype(jnp.int32)
    names = (first == me) | (second == me)
    other = jnp.where(first == me, second, first)
    routed = 1.0 / (1.0 + jnp.exp(pick(logits, other) - pick(logits, me)))
    naming = jnp.broadcast_to(jnp.where(names, 1.0, 0.0), (TOKENS, 128))
    place = row % OWNED
    earlier = jnp.where(place >= 1, pltpu.roll(naming, 1, 0), 0.0)
    earlier += jnp.where(place >= 2, pltpu.roll(naming, 2, 0), 0.0)
    earlier = earlier[:, :1]
    kept = names & (earlier < capacity_ref[me].astype(f32))
    weight = jnp.where(kept, routed, 0.0)
    gate, up = gate * scale, up * scale
    inner = (gate / (1.0 + jnp.exp(-gate)) * up * weight).astype(bf16)
    for k in range(CHIPS):
        y = jnp.dot(inner, down_ref[:, 2 * COLS * k : 2 * COLS * (k + 1)], preferred_element_type=f32)
        even, odd = y[:, :COLS], y[:, COLS:]
        keep_ref[k] = jnp.where(core == 0, even, odd)
        send_ref[k] = jnp.where(core == 0, odd, even).astype(bf16)


def pair_kernel(keep_ref, got_ref, out_ref):
    for k in range(CHIPS):
        total = (keep_ref[k] + got_ref[k].astype(f32)).astype(bf16).astype(f32)
        for e in range(EXPERTS):
            out_ref[EXPERTS * k + e] = total[OWNED * e : OWNED * (e + 1), :].astype(bf16)


def final_kernel(where_ref, in_ref, residual_ref, out_ref):
    me = where_ref[1]
    total = jnp.zeros((OWNED, COLS), f32)
    for e in range(EXPERTS):
        rows = residual_ref[OWNED * e : OWNED * (e + 1), :COLS]
        total += jnp.where(me == e, rows, 0.0)
    out_ref[...] = (total + jnp.sum(in_ref[...].astype(f32), axis=0)).astype(bf16)


def shaped(shape, dtype):
    return jax.ShapeDtypeStruct(shape, dtype)


def call(kernel, outs, specs, scratch=(), limit=None):
    single = not isinstance(outs, tuple)
    return pl.pallas_call(
        kernel,
        out_shape=outs,
        in_specs=list(specs),
        out_specs=VMEM if single else (VMEM,) * len(outs),
        scratch_shapes=list(scratch),
        compiler_params=pltpu.CompilerParams(vmem_limit_bytes=limit),
    )


def exchanged(value, axes):
    return lax.all_to_all(value, axes, 0, 0, tiled=True)


def swapped(value):
    return lax.ppermute(value, "seq_2", [(0, 1), (1, 0)])


def on_device(
    hidden_in,
    queries,
    key_cache,
    value_cache,
    lengths,
    out_weight,
    norm_gain,
    router,
    expert_ids,
    capacity,
    w_gate,
    w_up,
    w_down,
):
    span = key_cache.shape[1]
    where = jnp.stack(
        [lax.axis_index(SEQ) * span, lax.axis_index("exp"), lax.axis_index("seq_2")]
    ).astype(jnp.int32)
    partial = call(
        attention_kernel,
        shaped((8, HALF_ROWS, 128), bf16),
        (SMEM, SMEM, VMEM, ANY, ANY),
        (
            pltpu.VMEM(key_cache.shape, bf16),
            pltpu.VMEM(value_cache.shape, bf16),
            pltpu.VMEM((TOKENS * SUB, 128), f32),
            pltpu.SemaphoreType.DMA((2, CHUNKS)),
        ),
        limit=12 << 20,
    )(where, lengths, queries, key_cache, value_cache)
    partial = exchanged(partial, ("seq_0", "seq_2"))
    partial = call(merge_kernel, shaped((8, HALF_ROWS, 128), bf16), (VMEM,))(partial)
    partial = exchanged(partial, ("seq_1", "seq_2"))
    projected, rest = call(
        project_kernel,
        (shaped((8, TOKENS, 256), bf16), shaped((TOKENS, 256), f32)),
        (SMEM, SMEM, VMEM, VMEM, VMEM),
        (pltpu.VMEM((TOKENS * SUB, 128), f32), pltpu.VMEM((TOKENS, 256), f32)),
    )(where, expert_ids.T, partial, hidden_in, out_weight.T)
    projected = exchanged(projected, "exp")
    gained, residual = call(
        gained_kernel,
        (shaped((CHIPS, TOKENS, 256), bf16), shaped((TOKENS, 256), f32)),
        (VMEM,) * 4,
        (pltpu.VMEM((TOKENS, 256), f32),),
    )(projected, rest, norm_gain[None, :], router.T)
    own = exchanged(gained, ("seq_0", "seq_1"))
    other = swapped(own)
    keep, send = call(
        expert_kernel,
        (shaped((CHIPS, TOKENS, COLS), f32), shaped((CHIPS, TOKENS, COLS), bf16)),
        (SMEM, SMEM) + (VMEM,) * 6,
        limit=24 << 20,
    )(where, capacity, own, other, residual, w_gate[0], w_up[0], w_down[0])
    got = swapped(send)
    summed = call(pair_kernel, shaped((CHIPS * EXPERTS, OWNED, COLS), bf16), (VMEM, VMEM))(keep, got)
    summed = exchanged(summed, ("seq_0", "seq_1", "exp"))
    return call(final_kernel, shaped((OWNED, COLS), bf16), (SMEM, VMEM, VMEM))(where, summed, residual)


def solution(mesh):
    split = Mesh(
        mesh.devices.reshape(4, 4, 2, mesh.shape["exp"]), ("seq_0", "seq_1", "seq_2", "exp")
    )
    placed = (
        P("exp", SEQ),
        P(None, "exp"),
        P(None, SEQ, "exp"),
        P(None, SEQ, "exp"),
        P(),
        P("exp", SEQ),
        P(SEQ),
        P(SEQ, None),
        P("exp", None),
        P(),
        P("exp", None, SEQ),
        P("exp", None, SEQ),
        P("exp", SEQ, None),
    )
    return jax.shard_map(
        on_device, mesh=split, in_specs=placed, out_specs=P("exp", SEQ), check_vma=False
    )
```

```python
import functools
import math

import jax
import jax.numpy as jnp
from jax import lax
from jax.experimental import pallas as pl
from jax.experimental.pallas import tpu as pltpu
from jax.sharding import Mesh
from jax.sharding import PartitionSpec as P

D = 6144
HEADS = 48
KV_HEADS = 8
HEAD_DIM = 128
EXPERTS = 8
TOKENS = 24
OWNED = 3
GROUP = HEADS // KV_HEADS
COLS = 192
HALF = TOKENS // 2
SUB = 8
HALF_ROWS = HALF * SUB
CHIPS = 16
SEQ = ("seq_0", "seq_1", "seq_2")
masked_score = -1e30
norm_eps = 1e-05
f32 = jnp.float32
bf16 = jnp.bfloat16
VMEM = pl.BlockSpec(memory_space=pltpu.VMEM)
SMEM = pl.BlockSpec(memory_space=pltpu.SMEM)
HBM = pl.BlockSpec(memory_space=pltpu.HBM)


def lanes(shape):
    return lax.broadcasted_iota(jnp.int32, shape, len(shape) - 1)


def subs(shape):
    return lax.broadcasted_iota(jnp.int32, shape, len(shape) - 2)


def rounded(x):
    return x.astype(bf16).astype(f32)


CHUNKS = 4
PER = TOKENS // CHUNKS


def attention_kernel(lengths_any, q_any, k_any, v_any, out_ref, lengths_ref, q_ref, kbuf, vbuf, qs, sems):
    heads = pltpu.make_async_copy(q_any, q_ref, sems.at[2, 0])
    limits = pltpu.make_async_copy(lengths_any, lengths_ref, sems.at[2, 1])
    heads.start()
    limits.start()
    copies = []
    for i in range(CHUNKS):
        part = pl.ds(i * PER, PER)
        copies.append(
            (
                pltpu.make_async_copy(k_any.at[part], kbuf.at[part], sems.at[0, i]),
                pltpu.make_async_copy(v_any.at[part], vbuf.at[part], sems.at[1, i]),
            )
        )
    for pair in copies:
        pair[0].start()
        pair[1].start()
    qs[...] = jnp.zeros_like(qs)
    heads.wait()
    for h in range(GROUP):
        qs[pl.ds(h, TOKENS, stride=SUB), :] = q_ref[:, h * HEAD_DIM : (h + 1) * HEAD_DIM].astype(f32)
    limits.wait()
    span = k_any.shape[1]
    first = lax.axis_index(SEQ) * span
    places = first + lanes((SUB, span))
    lane, sub = lanes((SUB, 128)), subs((SUB, 128))
    scale = 1.0 / math.sqrt(HEAD_DIM)
    for i in range(CHUNKS):
        copies[i][0].wait()
        scores = []
        for b in range(i * PER, (i + 1) * PER):
            query = qs[b * SUB : (b + 1) * SUB, :].astype(bf16)
            s = lax.dot_general(query, kbuf[b], (((1,), (1,)), ((), ())), preferred_element_type=f32)
            scores.append(jnp.where(places < lengths_ref[b], s * scale, masked_score))
        copies[i][1].wait()
        blocks = []
        for n, b in enumerate(range(i * PER, (i + 1) * PER)):
            s = scores[n]
            peak = rounded(jnp.max(s, axis=-1, keepdims=True))
            p = jnp.where(places < lengths_ref[b], jnp.exp(s - peak), 0.0)
            total = jnp.sum(p, axis=-1, keepdims=True)
            p_hi = rounded(p)
            both = jnp.concatenate([p_hi, p - p_hi], axis=0).astype(bf16)
            weighted = jnp.dot(both, vbuf[b], preferred_element_type=f32)
            weighted = weighted[:SUB] + weighted[SUB:]
            total_hi = rounded(total)
            stats = jnp.where(lane == sub, peak, 0.0)
            stats = jnp.where(lane == sub + SUB, total_hi, stats)
            stats = jnp.where(lane == sub + 2 * SUB, total - total_hi, stats)
            stats = jnp.sum(jnp.where(sub < GROUP, stats, 0.0), axis=0, keepdims=True)
            blocks.append(jnp.where(sub == GROUP, stats, weighted))
        for n in range(0, PER, 2):
            b = i * PER + n
            half, row = b // HALF, (b % HALF) * SUB
            two = jnp.concatenate([blocks[n], blocks[n + 1]], axis=0).astype(bf16)
            for y in range(4):
                out_ref[2 * y + half, row : row + 2 * SUB, :] = two


def combined(blocks):
    shape = (HALF, SUB, 128)
    lane, sub = lanes(shape), subs(shape)
    flat = lanes((HALF, 1, 128))
    stats = [jnp.sum(jnp.where(sub == GROUP, x, 0.0), axis=1, keepdims=True) for x in blocks]
    peak = functools.reduce(jnp.maximum, stats)
    factors = [jnp.exp(jnp.minimum(s - peak, 0.0)) for s in stats]
    total = jnp.zeros((HALF, 1, 128), f32)
    for s, factor in zip(stats, factors):
        total += factor * (pltpu.roll(s, 128 - SUB, 2) + pltpu.roll(s, 128 - 2 * SUB, 2))
    total = jnp.where(flat < GROUP, total, 1.0)
    return peak, factors, total


def as_column(x):
    shape = (HALF, SUB, 128)
    wide = jnp.broadcast_to(x, shape)
    return jnp.sum(jnp.where(lanes(shape) == subs(shape), wide, 0.0), axis=2, keepdims=True)


def merge_kernel(in_ref, ahead_ref, out_ref):
    blocks = [in_ref[i].astype(f32).reshape(HALF, SUB, 128) for i in range(8)]
    peak, factors, total = combined(blocks)
    weighted = jnp.zeros((HALF, SUB, 128), f32)
    for x, factor in zip(blocks, factors):
        weighted += as_column(factor) * x
    flat = lanes((HALF, 1, 128))
    total_hi = rounded(total)
    stats = jnp.where(flat < SUB, peak, pltpu.roll(total_hi, SUB, 2))
    stats = jnp.where(flat < 2 * SUB, stats, pltpu.roll(total - total_hi, 2 * SUB, 2))
    stats = jnp.where(flat < 3 * SUB, stats, 0.0)
    sub = subs((HALF, SUB, 128))
    block = jnp.where(sub == GROUP, stats, weighted).reshape(HALF_ROWS, 128).astype(bf16)
    for i in range(8):
        out_ref[i] = block


def project_kernel(ids_ref, in_ref, hidden_ref, weight_ref, ahead_ref, out_ref, rest_ref, att, wide):
    for half in range(2):
        blocks = [in_ref[2 * z + half].astype(f32).reshape(HALF, SUB, 128) for z in range(4)]
        _, factors, total = combined(blocks)
        inverse = 1.0 / total
        weighted = jnp.zeros((HALF, SUB, 128), f32)
        for x, factor in zip(blocks, factors):
            weighted += as_column(factor * inverse) * x
        att[half * HALF_ROWS : (half + 1) * HALF_ROWS, :] = weighted.reshape(HALF_ROWS, 128)
    acc = jnp.zeros((TOKENS, COLS), f32)
    for h in range(GROUP):
        rows = att[pl.ds(h, TOKENS, stride=SUB), :].astype(bf16)
        acc += lax.dot_general(
            rows,
            weight_ref[:, h * HEAD_DIM : (h + 1) * HEAD_DIM],
            (((1,), (1,)), ((), ())),
            preferred_element_type=f32,
        )
    mine = OWNED * lax.axis_index("exp")
    row = subs((TOKENS, COLS))
    hidden = hidden_ref[...].astype(f32)
    for r in range(OWNED):
        acc += jnp.where(row == mine + r, hidden[r : r + 1, :], 0.0)
    tail = jnp.zeros((TOKENS, 64), f32)
    lane, row_tail = lanes((TOKENS, 64)), subs((TOKENS, 64))
    for r in range(OWNED):
        for k in range(2):
            here = (row_tail == mine + r) & (lane == k)
            tail = jnp.where(here, ids_ref[k, r].astype(f32), tail)
    wide[:, :COLS] = acc
    wide[:, COLS:] = tail
    full = wide[...]
    sent = full.astype(bf16)
    for i in range(8):
        out_ref[i] = sent
    row = subs((TOKENS, 256))
    owned = (row >= mine) & (row < mine + OWNED)
    rest_ref[...] = jnp.where(owned, full - sent.astype(f32), 0.0)


def gained_kernel(in_ref, rest_ref, gain_ref, router_ref, ahead_ref, out_ref, residual_ref, wide):
    total = rest_ref[...]
    for i in range(8):
        total += in_ref[i].astype(f32)
    residual_ref[...] = total
    residual = total[:, :COLS]
    gained = residual * gain_ref[...]
    hi = gained.astype(bf16)
    lo = (gained - hi.astype(f32)).astype(bf16)
    over_features = (((1,), (1,)), ((), ()))
    logits = lax.dot_general(hi, router_ref[...], over_features, preferred_element_type=f32)
    logits += lax.dot_general(lo, router_ref[...], over_features, preferred_element_type=f32)
    squares = jnp.sum(residual * residual, axis=-1, keepdims=True)
    logits_hi, squares_hi = rounded(logits), rounded(squares)
    wide[...] = jnp.zeros_like(wide)
    wide[:, :COLS] = gained
    wide[:, COLS : COLS + 8] = logits_hi
    wide[:, COLS + 8 : COLS + 9] = squares_hi
    wide[:, COLS + 32 : COLS + 40] = logits - logits_hi
    wide[:, COLS + 40 : COLS + 41] = squares - squares_hi
    sent = wide[...].astype(bf16)
    for i in range(CHIPS):
        out_ref[i] = sent


def expert_kernel(
    capacity_ref, own_ref, other_ref, residual_ref, gate_ref, up_ref, down_ref, keep_ref, send_ref
):
    core, me = lax.axis_index("seq_2"), lax.axis_index("exp")
    stats = jnp.zeros((TOKENS, 128), f32)
    gate = jnp.zeros((TOKENS, 256), f32)
    up = jnp.zeros((TOKENS, 256), f32)
    for k in range(CHIPS):
        for ref, parity in ((own_ref, core), (other_ref, 1 - core)):
            stats += ref[k, :, 128:].astype(f32)
            rows = pl.ds(pl.multiple_of((2 * k + parity) * COLS, COLS), COLS)
            x = ref[k, :, :COLS]
            gate += jnp.dot(x, gate_ref[rows, :], preferred_element_type=f32)
            up += jnp.dot(x, up_ref[rows, :], preferred_element_type=f32)
    stats = pltpu.roll(stats, 64, 1) + pltpu.roll(stats, 32, 1)
    lane, row = lanes((TOKENS, 128)), subs((TOKENS, 128))

    def pick(x, place):
        return jnp.sum(jnp.where(lane == place, x, 0.0), axis=-1, keepdims=True)

    scale = lax.rsqrt(pick(stats, 8) / D + norm_eps)
    logits = stats * scale
    named = residual_ref[:, 128:]
    first, second = pick(named, 64).astype(jnp.int32), pick(named, 65).astype(jnp.int32)
    names = (first == me) | (second == me)
    other = jnp.where(first == me, second, first)
    routed = 1.0 / (1.0 + jnp.exp(pick(logits, other) - pick(logits, me)))
    naming = jnp.broadcast_to(jnp.where(names, 1.0, 0.0), (TOKENS, 128))
    place = row % OWNED
    earlier = jnp.where(place >= 1, pltpu.roll(naming, 1, 0), 0.0)
    earlier += jnp.where(place >= 2, pltpu.roll(naming, 2, 0), 0.0)
    earlier = earlier[:, :1]
    kept = names & (earlier < capacity_ref[me].astype(f32))
    weight = jnp.where(kept, routed, 0.0)
    gate, up = gate * scale, up * scale
    inner = (gate / (1.0 + jnp.exp(-gate)) * up * weight).astype(bf16)
    for k in range(CHIPS):
        y = jnp.dot(inner, down_ref[:, 2 * COLS * k : 2 * COLS * (k + 1)], preferred_element_type=f32)
        even, odd = y[:, :COLS], y[:, COLS:]
        keep_ref[k] = jnp.where(core == 0, even, odd)
        send_ref[k] = jnp.where(core == 0, odd, even).astype(bf16)


def pair_kernel(keep_ref, got_ref, out_ref):
    for k in range(CHIPS):
        total = (keep_ref[k] + got_ref[k].astype(f32)).astype(bf16).astype(f32)
        for e in range(EXPERTS):
            out_ref[EXPERTS * k + e] = total[OWNED * e : OWNED * (e + 1), :].astype(bf16)


def final_kernel(in_ref, residual_ref, out_ref):
    me = lax.axis_index("exp")
    total = jnp.zeros((OWNED, COLS), f32)
    for e in range(EXPERTS):
        rows = residual_ref[OWNED * e : OWNED * (e + 1), :COLS]
        total += jnp.where(me == e, rows, 0.0)
    out_ref[...] = (total + jnp.sum(in_ref[...].astype(f32), axis=0)).astype(bf16)


def shaped(shape, dtype):
    return jax.ShapeDtypeStruct(shape, dtype)


def call(kernel, outs, specs, scratch=(), limit=6 << 20):
    single = not isinstance(outs, tuple)
    return pl.pallas_call(
        kernel,
        out_shape=outs,
        in_specs=list(specs),
        out_specs=VMEM if single else (VMEM,) * len(outs),
        scratch_shapes=list(scratch),
        compiler_params=pltpu.CompilerParams(vmem_limit_bytes=limit),
        cost_estimate=pl.CostEstimate(flops=1 << 20, bytes_accessed=1 << 20, transcendentals=0),
    )


def exchanged(value, axes):
    return lax.all_to_all(value, axes, 0, 0, tiled=True)


def swapped(value):
    return lax.ppermute(value, "seq_2", [(0, 1), (1, 0)])


def on_device(
    hidden_in,
    queries,
    key_cache,
    value_cache,
    lengths,
    out_weight,
    norm_gain,
    router,
    expert_ids,
    capacity,
    w_gate,
    w_up,
    w_down,
):
    partial = call(
        attention_kernel,
        shaped((8, HALF_ROWS, 128), bf16),
        (HBM, HBM, HBM, HBM),
        (
            pltpu.SMEM(lengths.shape, jnp.int32),
            pltpu.VMEM(queries.shape, bf16),
            pltpu.VMEM(key_cache.shape, bf16),
            pltpu.VMEM(value_cache.shape, bf16),
            pltpu.VMEM((TOKENS * SUB, 128), f32),
            pltpu.SemaphoreType.DMA((3, CHUNKS)),
        ),
        limit=60 << 20,
    )(lengths, queries, key_cache, value_cache)
    partial = exchanged(partial, ("seq_0", "seq_2"))
    partial = call(merge_kernel, shaped((8, HALF_ROWS, 128), bf16), (VMEM, VMEM))(partial, w_gate)
    partial = exchanged(partial, ("seq_1", "seq_2"))
    projected, rest = call(
        project_kernel,
        (shaped((8, TOKENS, 256), bf16), shaped((TOKENS, 256), f32)),
        (SMEM, VMEM, VMEM, VMEM, VMEM),
        (pltpu.VMEM((TOKENS * SUB, 128), f32), pltpu.VMEM((TOKENS, 256), f32)),
    )(expert_ids.T, partial, hidden_in, out_weight.T, w_up)
    projected = exchanged(projected, "exp")
    gained, residual = call(
        gained_kernel,
        (shaped((CHIPS, TOKENS, 256), bf16), shaped((TOKENS, 256), f32)),
        (VMEM,) * 5,
        (pltpu.VMEM((TOKENS, 256), f32),),
    )(projected, rest, norm_gain[None, :], router.T, w_down)
    own = exchanged(gained, ("seq_0", "seq_1"))
    other = swapped(own)
    keep, send = call(
        expert_kernel,
        (shaped((CHIPS, TOKENS, COLS), f32), shaped((CHIPS, TOKENS, COLS), bf16)),
        (SMEM,) + (VMEM,) * 6,
        limit=14 << 20,
    )(capacity, own, other, residual, w_gate[0], w_up[0], w_down[0])
    got = swapped(send)
    summed = call(pair_kernel, shaped((CHIPS * EXPERTS, OWNED, COLS), bf16), (VMEM, VMEM))(keep, got)
    summed = exchanged(summed, ("seq_0", "seq_1", "exp"))
    return call(final_kernel, shaped((OWNED, COLS), bf16), (VMEM, VMEM))(summed, residual)


def solution(mesh):
    split = Mesh(
        mesh.devices.reshape(4, 4, 2, mesh.shape["exp"]), ("seq_0", "seq_1", "seq_2", "exp")
    )
    placed = (
        P("exp", SEQ),
        P(None, "exp"),
        P(None, SEQ, "exp"),
        P(None, SEQ, "exp"),
        P(),
        P("exp", SEQ),
        P(SEQ),
        P(SEQ, None),
        P("exp", None),
        P(),
        P("exp", None, SEQ),
        P("exp", None, SEQ),
        P("exp", SEQ, None),
    )
    return jax.shard_map(
        on_device, mesh=split, in_specs=placed, out_specs=P("exp", SEQ), check_vma=False
    )
```

```python
import functools
import math

import jax
import jax.numpy as jnp
from jax import lax
from jax.experimental import pallas as pl
from jax.experimental.pallas import tpu as pltpu
from jax.sharding import Mesh
from jax.sharding import PartitionSpec as P

D = 6144
HEADS = 48
KV_HEADS = 8
HEAD_DIM = 128
EXPERTS = 8
TOKENS = 24
OWNED = 3
GROUP = HEADS // KV_HEADS
COLS = 192
HALF = TOKENS // 2
SUB = 8
HALF_ROWS = HALF * SUB
CHIPS = 16
SEQ = ("seq_0", "seq_1", "seq_2")
masked_score = -1e30
norm_eps = 1e-05
f32 = jnp.float32
bf16 = jnp.bfloat16
VMEM = pl.BlockSpec(memory_space=pltpu.VMEM)
SMEM = pl.BlockSpec(memory_space=pltpu.SMEM)
HBM = pl.BlockSpec(memory_space=pltpu.HBM)


def lanes(shape):
    return lax.broadcasted_iota(jnp.int32, shape, len(shape) - 1)


def subs(shape):
    return lax.broadcasted_iota(jnp.int32, shape, len(shape) - 2)


def rounded(x):
    return x.astype(bf16).astype(f32)


CHUNKS = 4
PER = TOKENS // CHUNKS
BOTH = 2 * COLS
PACKED = HALF * GROUP
BLOCK = PACKED + SUB
ROWS = 16


def attention_kernel(
    lengths_any, q_any, k_any, v_any, hidden_ref, router_ref, gain_ref,
    keep_ref, send_ref, small_ref,
    lengths_ref, q_ref, kbuf, vbuf, qs, halves, sems,
):
    heads = pltpu.make_async_copy(q_any, q_ref, sems.at[2, 0])
    limits = pltpu.make_async_copy(lengths_any, lengths_ref, sems.at[2, 1])
    heads.start()
    limits.start()
    copies = []
    for i in range(CHUNKS):
        part = pl.ds(i * PER, PER)
        copies.append(
            (
                pltpu.make_async_copy(k_any.at[part], kbuf.at[part], sems.at[0, i]),
                pltpu.make_async_copy(v_any.at[part], vbuf.at[part], sems.at[1, i]),
            )
        )
    for pair in copies:
        pair[0].start()
        pair[1].start()
    gain = gain_ref[...]
    gain_hi = rounded(gain)
    gain_mid = rounded(gain - gain_hi)
    row = subs((ROWS, COLS))
    small = jnp.zeros((ROWS, COLS), f32)
    hidden, router = hidden_ref[...].astype(f32), router_ref[...].astype(f32)
    lines = [hidden[r : r + 1] for r in range(OWNED)] + [router[r : r + 1] for r in range(EXPERTS)]
    for r, line in enumerate(lines + [gain_hi, gain_mid, gain - gain_hi - gain_mid]):
        small = jnp.where(row == r, line, small)
    small_ref[...] = small.astype(bf16)
    qs[...] = jnp.zeros_like(qs)
    heads.wait()
    for h in range(GROUP):
        qs[pl.ds(h, TOKENS, stride=SUB), :] = q_ref[:, h * HEAD_DIM : (h + 1) * HEAD_DIM].astype(f32)
    limits.wait()
    span = k_any.shape[1]
    first = lax.axis_index(SEQ) * span
    places = first + lanes((SUB, span))
    lane, sub = lanes((SUB, 128)), subs((SUB, 128))
    scale = 1.0 / math.sqrt(HEAD_DIM)
    for i in range(CHUNKS):
        copies[i][0].wait()
        scores = []
        for b in range(i * PER, (i + 1) * PER):
            query = qs[b * SUB : (b + 1) * SUB, :].astype(bf16)
            s = lax.dot_general(query, kbuf[b], (((1,), (1,)), ((), ())), preferred_element_type=f32)
            scores.append(jnp.where(places < lengths_ref[b], s * scale, masked_score))
        copies[i][1].wait()
        for n, b in enumerate(range(i * PER, (i + 1) * PER)):
            s = scores[n]
            peak = rounded(jnp.max(s, axis=-1, keepdims=True))
            p = jnp.where(places < lengths_ref[b], jnp.exp(s - peak), 0.0)
            total = jnp.sum(p, axis=-1, keepdims=True)
            p_hi = rounded(p)
            both = jnp.concatenate([p_hi, p - p_hi], axis=0).astype(bf16)
            weighted = jnp.dot(both, vbuf[b], preferred_element_type=f32)
            weighted = weighted[:SUB] + weighted[SUB:]
            stats = jnp.where(lane == sub, peak, 0.0)
            stats = jnp.where(lane == sub + SUB, total, stats)
            stats = jnp.sum(jnp.where(sub < GROUP, stats, 0.0), axis=0, keepdims=True)
            half, line = b // HALF, (b % HALF) * SUB
            halves[half, line : line + SUB, :] = jnp.where(sub == GROUP, stats, weighted)
    core = lax.axis_index("seq_2")
    keep_ref[...] = halves[core]
    send_ref[...] = halves[1 - core]


def as_column(x):
    shape = (HALF, SUB, 128)
    wide = jnp.broadcast_to(x, shape)
    return jnp.sum(jnp.where(lanes(shape) == subs(shape), wide, 0.0), axis=2, keepdims=True)


def merge_kernel(keep_ref, got_ref, weight_ref, small_ref, ahead_ref, out_ref, packed):
    shape = (HALF, SUB, 128)
    sub = subs(shape)
    blocks = [ref[...].reshape(shape) for ref in (keep_ref, got_ref)]
    stats = [jnp.sum(jnp.where(sub == GROUP, x, 0.0), axis=1, keepdims=True) for x in blocks]
    peak = jnp.maximum(stats[0], stats[1])
    weighted, total = jnp.zeros(shape, f32), jnp.zeros((HALF, 1, 128), f32)
    for x, s in zip(blocks, stats):
        factor = jnp.exp(jnp.minimum(s - peak, 0.0))
        total += factor * pltpu.roll(s, 128 - SUB, 2)
        weighted += as_column(factor) * x
    flat = lanes((HALF, 1, 128))
    total_hi = rounded(total)
    line = jnp.where(flat < SUB, peak, pltpu.roll(total_hi, SUB, 2))
    line = jnp.where(flat < 2 * SUB, line, pltpu.roll(total - total_hi, 2 * SUB, 2))
    line = jnp.where(flat % SUB < GROUP, jnp.where(flat < 3 * SUB, line, 0.0), 0.0)
    tile, row, lane = jnp.zeros((SUB, 128), f32), subs((SUB, 128)), lanes((SUB, 128))
    for t in range(HALF):
        packed[GROUP * t : GROUP * (t + 1), :] = weighted[t, :GROUP, :]
        here = (row == t % SUB) & (lane // 32 == t // SUB)
        value = line[t] if t < SUB else pltpu.roll(line[t], 32, 1)
        tile = jnp.where(here, value, tile)
    packed[PACKED:, :] = tile
    block = packed[...].astype(bf16)
    for i in range(CHIPS):
        out_ref[i] = block


def project_kernel(
    ids_ref, in_ref, hidden_ref, small_ref, weight_ref, other_ref, ahead_ref, out_ref, rest_ref, att, wide
):
    core, me = lax.axis_index("seq_2"), lax.axis_index("exp")
    tiles = [in_ref[i, PACKED:, :].astype(f32) for i in range(CHIPS)]
    peak = functools.reduce(jnp.maximum, tiles)
    factors = [jnp.exp(jnp.minimum(s - peak, 0.0)) for s in tiles]
    total = jnp.zeros((SUB, 128), f32)
    for s, factor in zip(tiles, factors):
        total += factor * (pltpu.roll(s, 128 - SUB, 1) + pltpu.roll(s, 128 - 2 * SUB, 1))
    lane = lanes((SUB, 128))
    inverse = 1.0 / jnp.where((lane % 32 < GROUP) & (total > 0.0), total, 1.0)
    row = lax.broadcasted_iota(jnp.int32, (PACKED, 2 * SUB), 0)
    column = lax.broadcasted_iota(jnp.int32, (PACKED, 2 * SUB), 1)
    spread = jnp.where((row // GROUP) % SUB == column % SUB, 1.0, 0.0).astype(bf16)
    row = subs((PACKED, 128))
    wanted = lanes((PACKED, 128)) == 32 * (row // GROUP // SUB) + row % GROUP
    weighted = jnp.zeros((PACKED, 128), f32)
    for i in range(CHIPS):
        factor = factors[i] * inverse
        factor_hi = rounded(factor)
        parts = jnp.concatenate([factor_hi, factor - factor_hi], axis=0).astype(bf16)
        wide_factor = jnp.dot(spread, parts, preferred_element_type=f32)
        factor = jnp.sum(jnp.where(wanted, wide_factor, 0.0), axis=-1, keepdims=True)
        weighted += factor * in_ref[i, :PACKED, :].astype(f32)
    att[:PACKED, :] = weighted
    acc, acc_other = jnp.zeros((HALF, COLS), f32), jnp.zeros((HALF, COLS), f32)
    over_features = (((1,), (1,)), ((), ()))
    for h in range(GROUP):
        rows = att[pl.ds(h, HALF, stride=GROUP), :].astype(bf16)
        cols = slice(h * HEAD_DIM, (h + 1) * HEAD_DIM)
        acc += lax.dot_general(rows, weight_ref[:, cols], over_features, preferred_element_type=f32)
        acc_other += lax.dot_general(rows, other_ref[:, cols], over_features, preferred_element_type=f32)
    mine = OWNED * me - HALF * core
    row = subs((HALF, COLS))
    hidden, hidden_other = hidden_ref[...].astype(f32), small_ref[...].astype(f32)
    for r in range(OWNED):
        acc += jnp.where(row == mine + r, hidden[r : r + 1, :], 0.0)
        acc_other += jnp.where(row == mine + r, hidden_other[r : r + 1, :], 0.0)
    row, lane = subs((ROWS, BOTH)), lanes((ROWS, BOTH))
    ids = jnp.zeros((ROWS, BOTH), f32)
    for r in range(OWNED):
        for k in range(2):
            here = (row == HALF) & (lane == 2 * (OWNED * me + r) + k)
            ids = jnp.where(here, ids_ref[k, r].astype(f32), ids)
    wide[...] = ids
    wide[:HALF, :COLS] = jnp.where(core == 0, acc, acc_other)
    wide[:HALF, COLS:] = jnp.where(core == 0, acc_other, acc)
    full = wide[...]
    sent = full.astype(bf16)
    for i in range(EXPERTS):
        out_ref[i] = sent
    owned = (row >= mine) & (row < mine + OWNED) & (row < HALF)
    rest_ref[...] = jnp.where(owned, full - sent.astype(f32), 0.0)


def gained_kernel(in_ref, rest_ref, gain_ref, router_ref, small_ref, ahead_ref, out_ref, residual_ref, wide):
    core = lax.axis_index("seq_2")
    total = rest_ref[...]
    for i in range(EXPERTS):
        total += in_ref[i].astype(f32)
    residual_ref[...] = total
    small = small_ref[...].astype(f32)
    router, router_other = router_ref[...].astype(f32), small[OWNED : OWNED + EXPERTS]
    gain = gain_ref[...]
    gain_other = small[11:12] + (small[12:13] + small[13:14])
    wide[:EXPERTS, :COLS] = jnp.where(core == 0, router, router_other)
    wide[:EXPERTS, COLS:] = jnp.where(core == 0, router_other, router)
    wide[EXPERTS : EXPERTS + 1, :COLS] = jnp.where(core == 0, gain, gain_other)
    wide[EXPERTS : EXPERTS + 1, COLS:] = jnp.where(core == 0, gain_other, gain)
    routers = wide[:EXPERTS, :].astype(bf16)
    row = subs((ROWS, BOTH))
    residual = jnp.where(row < HALF, total, 0.0)
    gained = residual * wide[EXPERTS : EXPERTS + 1, :]
    hi = gained.astype(bf16)
    lo = (gained - hi.astype(f32)).astype(bf16)
    over_features = (((1,), (1,)), ((), ()))
    logits = lax.dot_general(hi, routers, over_features, preferred_element_type=f32)
    logits += lax.dot_general(lo, routers, over_features, preferred_element_type=f32)
    squares = jnp.sum(residual * residual, axis=-1, keepdims=True)
    logits_hi, squares_hi = rounded(logits), rounded(squares)
    wide[:, :128] = jnp.zeros((ROWS, 128), f32)
    wide[:, :8] = logits_hi
    wide[:, 8:9] = squares_hi
    wide[:, 16:24] = logits - logits_hi
    wide[:, 24:25] = squares - squares_hi
    stats = wide[:, :128].astype(bf16)
    to = lax.broadcasted_iota(jnp.int32, (ROWS, ROWS), 0)
    source = lax.broadcasted_iota(jnp.int32, (ROWS, ROWS), 1)
    row = subs((ROWS, 128))
    for j in range(3):
        choice = jnp.where((to >= HALF) & (source == 3 * (to - HALF) + j), 1.0, 0.0).astype(bf16)
        packed = jnp.dot(choice, stats, preferred_element_type=f32)
        cols = slice(128 * j, 128 * (j + 1))
        sent = jnp.where(row < HALF, gained[:, cols], packed).astype(bf16)
        for i in range(CHIPS):
            out_ref[i, :, cols] = sent


def expert_kernel(
    capacity_ref, own_ref, other_ref, residual_ref, gate_ref, up_ref, down_ref, keep_ref, send_ref
):
    core, me = lax.axis_index("seq_2"), lax.axis_index("exp")
    sums = [jnp.zeros((ROWS, BOTH), f32) for _ in range(2)]
    gate = jnp.zeros((2 * ROWS, 256), f32)
    up = jnp.zeros((2 * ROWS, 256), f32)
    for k in range(CHIPS):
        own, other = own_ref[k], other_ref[k]
        pair = (jnp.where(core == 0, own, other), jnp.where(core == 0, other, own))
        for i in range(2):
            sums[i] += pair[i].astype(f32)
        x = jnp.concatenate(pair, axis=0)
        rows = slice(BOTH * k, BOTH * (k + 1))
        gate += jnp.dot(x, gate_ref[rows, :], preferred_element_type=f32)
        up += jnp.dot(x, up_ref[rows, :], preferred_element_type=f32)
    shape = (2 * ROWS, 128)
    lane, row = lanes(shape), subs(shape)
    stats = jnp.zeros(shape, f32)
    for half in range(2):
        for t in range(HALF):
            line = sums[half][HALF + t // 3 : HALF + t // 3 + 1, 128 * (t % 3) : 128 * (t % 3 + 1)]
            stats = jnp.where(row == ROWS * half + t, line, stats)
    stats += pltpu.roll(stats, 128 - 16, 1)

    def pick(x, place):
        return jnp.sum(jnp.where(lane == place, x, 0.0), axis=-1, keepdims=True)

    scale = lax.rsqrt(pick(stats, 8) / D + norm_eps)
    logits = stats * scale
    inside = row % ROWS
    token = HALF * (row // ROWS) + inside
    named = jnp.broadcast_to(residual_ref[HALF : HALF + 1, :128], shape)
    first, second = pick(named, 2 * token).astype(jnp.int32), pick(named, 2 * token + 1).astype(jnp.int32)
    names = (first == me) | (second == me)
    other = jnp.where(first == me, second, first)
    routed = 1.0 / (1.0 + jnp.exp(pick(logits, other) - pick(logits, me)))
    naming = jnp.broadcast_to(jnp.where(names, 1.0, 0.0), shape)
    place = inside % OWNED
    earlier = jnp.where(place >= 1, pltpu.roll(naming, 1, 0), 0.0)
    earlier += jnp.where(place >= 2, pltpu.roll(naming, 2, 0), 0.0)
    kept = names & (earlier[:, :1] < capacity_ref[me].astype(f32)) & (inside[:, :1] < HALF)
    weight = jnp.where(kept, routed, 0.0)
    gate, up = gate * scale, up * scale
    inner = (gate / (1.0 + jnp.exp(-gate)) * up * weight).astype(bf16)
    for k in range(CHIPS):
        y = jnp.dot(inner, down_ref[:, BOTH * k : BOTH * (k + 1)], preferred_element_type=f32)
        even, odd = y[:, :COLS], y[:, COLS:]
        keep_ref[k] = jnp.where(core == 0, even, odd)
        send_ref[k] = jnp.where(core == 0, odd, even).astype(bf16)
    residual = residual_ref[...]
    residual = jnp.where(core == 0, residual[:, COLS:], residual[:, :COLS])
    residual_hi = residual.astype(bf16)
    send_ref[CHIPS, :ROWS, :] = residual_hi
    send_ref[CHIPS, ROWS:, :] = (residual - residual_hi.astype(f32)).astype(bf16)


def pair_kernel(keep_ref, got_ref, out_ref):
    for k in range(CHIPS):
        total = keep_ref[k] + got_ref[k].astype(f32)
        for e in range(EXPERTS):
            line = ROWS * (e // 4) + OWNED * (e % 4)
            out_ref[EXPERTS * k + e] = total[line : line + OWNED, :].astype(bf16)


def final_kernel(in_ref, residual_ref, got_ref, out_ref):
    core, me = lax.axis_index("seq_2"), lax.axis_index("exp")
    residual = residual_ref[...]
    own = jnp.where(core == 0, residual[:, :COLS], residual[:, COLS:])
    got = got_ref[CHIPS].astype(f32)
    residual = jnp.where(me // 4 == core, own, got[:ROWS] + got[ROWS:])
    total = jnp.zeros((OWNED, COLS), f32)
    for q in range(4):
        total += jnp.where(me % 4 == q, residual[OWNED * q : OWNED * (q + 1), :], 0.0)
    out_ref[...] = (total + jnp.sum(in_ref[...].astype(f32), axis=0)).astype(bf16)


def shaped(shape, dtype):
    return jax.ShapeDtypeStruct(shape, dtype)


def call(kernel, outs, specs, scratch=(), limit=6 << 20):
    single = not isinstance(outs, tuple)
    return pl.pallas_call(
        kernel,
        out_shape=outs,
        in_specs=list(specs),
        out_specs=VMEM if single else (VMEM,) * len(outs),
        scratch_shapes=list(scratch),
        compiler_params=pltpu.CompilerParams(vmem_limit_bytes=limit),
        cost_estimate=pl.CostEstimate(flops=1 << 20, bytes_accessed=1 << 20, transcendentals=0),
    )


def exchanged(value, axes):
    return lax.all_to_all(value, axes, 0, 0, tiled=True)


def swapped(value):
    return lax.ppermute(value, "seq_2", [(0, 1), (1, 0)])


def on_device(
    hidden_in,
    queries,
    key_cache,
    value_cache,
    lengths,
    out_weight,
    norm_gain,
    router,
    expert_ids,
    capacity,
    w_gate,
    w_up,
    w_down,
):
    keep, send, small = call(
        attention_kernel,
        (
            shaped((HALF_ROWS, 128), f32),
            shaped((HALF_ROWS, 128), f32),
            shaped((ROWS, COLS), bf16),
        ),
        (HBM, HBM, HBM, HBM, VMEM, VMEM, VMEM),
        (
            pltpu.SMEM(lengths.shape, jnp.int32),
            pltpu.VMEM(queries.shape, bf16),
            pltpu.VMEM(key_cache.shape, bf16),
            pltpu.VMEM(value_cache.shape, bf16),
            pltpu.VMEM((TOKENS * SUB, 128), f32),
            pltpu.VMEM((2, HALF_ROWS, 128), f32),
            pltpu.SemaphoreType.DMA((3, CHUNKS)),
        ),
        limit=60 << 20,
    )(lengths, queries, key_cache, value_cache, hidden_in, router.T, norm_gain[None, :])
    weight = out_weight.T
    weight_other = swapped(weight)
    got, small = swapped(send), swapped(small)
    partial = call(
        merge_kernel,
        shaped((CHIPS, BLOCK, 128), bf16),
        (VMEM,) * 5,
        (pltpu.VMEM((BLOCK, 128), f32),),
    )(keep, got, weight_other, small, w_gate)
    partial = exchanged(partial, ("seq_0", "seq_1"))
    projected, rest = call(
        project_kernel,
        (shaped((EXPERTS, ROWS, BOTH), bf16), shaped((ROWS, BOTH), f32)),
        (SMEM,) + (VMEM,) * 6,
        (pltpu.VMEM((BLOCK, 128), f32), pltpu.VMEM((ROWS, BOTH), f32)),
    )(expert_ids.T, partial, hidden_in, small, weight, weight_other, w_up)
    projected = exchanged(projected, "exp")
    gained, residual = call(
        gained_kernel,
        (shaped((CHIPS, ROWS, BOTH), bf16), shaped((ROWS, BOTH), f32)),
        (VMEM,) * 6,
        (pltpu.VMEM((ROWS, BOTH), f32),),
    )(projected, rest, norm_gain[None, :], router.T, small, w_down)
    own = exchanged(gained, ("seq_0", "seq_1"))
    other = swapped(own)
    keep, send = call(
        expert_kernel,
        (shaped((CHIPS, 2 * ROWS, COLS), f32), shaped((CHIPS + 1, 2 * ROWS, COLS), bf16)),
        (SMEM,) + (VMEM,) * 6,
        limit=14 << 20,
    )(capacity, own, other, residual, w_gate[0], w_up[0], w_down[0])
    got = swapped(send)
    summed = call(pair_kernel, shaped((CHIPS * EXPERTS, OWNED, COLS), bf16), (VMEM, VMEM))(keep, got)
    summed = exchanged(summed, ("seq_0", "seq_1", "exp"))
    return call(final_kernel, shaped((OWNED, COLS), bf16), (VMEM, VMEM, VMEM))(summed, residual, got)


def solution(mesh):
    split = Mesh(
        mesh.devices.reshape(4, 4, 2, mesh.shape["exp"]), ("seq_0", "seq_1", "seq_2", "exp")
    )
    placed = (
        P("exp", SEQ),
        P(None, "exp"),
        P(None, SEQ, "exp"),
        P(None, SEQ, "exp"),
        P(),
        P("exp", SEQ),
        P(SEQ),
        P(SEQ, None),
        P("exp", None),
        P(),
        P("exp", None, SEQ),
        P("exp", None, SEQ),
        P("exp", SEQ, None),
    )
    return jax.shard_map(
        on_device, mesh=split, in_specs=placed, out_specs=P("exp", SEQ), check_vma=False
    )
```

```python
import functools
import math

import jax
import jax.numpy as jnp
from jax import lax
from jax.experimental import pallas as pl
from jax.experimental.pallas import tpu as pltpu
from jax.sharding import Mesh
from jax.sharding import PartitionSpec as P

D = 6144
HEADS = 48
KV_HEADS = 8
HEAD_DIM = 128
EXPERTS = 8
TOKENS = 24
OWNED = 3
GROUP = HEADS // KV_HEADS
COLS = 192
HALF = TOKENS // 2
SUB = 8
HALF_ROWS = HALF * SUB
CHIPS = 16
SEQ = ("seq_0", "seq_1", "seq_2")
masked_score = -1e30
norm_eps = 1e-05
f32 = jnp.float32
bf16 = jnp.bfloat16
VMEM = pl.BlockSpec(memory_space=pltpu.VMEM)
SMEM = pl.BlockSpec(memory_space=pltpu.SMEM)


def lanes(shape):
    return lax.broadcasted_iota(jnp.int32, shape, len(shape) - 1)


def subs(shape):
    return lax.broadcasted_iota(jnp.int32, shape, len(shape) - 2)


def rounded(x):
    return x.astype(bf16).astype(f32)


CHUNKS = 4
PER = TOKENS // CHUNKS
BOTH = 2 * COLS
PACKED = HALF * GROUP
BLOCK = PACKED + SUB
ROWS = 16


def attention_kernel(
    lengths_ref, q_ref, k_ref, v_ref, hidden_ref, router_ref, gain_ref,
    keep_ref, send_ref, qs, halves,
):
    send_ref[HALF_ROWS:, :] = jnp.zeros((2 * ROWS, 128), f32)
    first = HALF_ROWS
    for ref in (hidden_ref, router_ref, gain_ref):
        lines = ref[...].astype(f32)
        send_ref[first : first + len(lines), :] = lines[:, :128]
        send_ref[first + ROWS : first + ROWS + len(lines), : COLS - 128] = lines[:, 128:]
        first += len(lines)
    qs[...] = jnp.zeros_like(qs)
    for h in range(GROUP):
        qs[pl.ds(h, TOKENS, stride=SUB), :] = q_ref[:, h * HEAD_DIM : (h + 1) * HEAD_DIM].astype(f32)
    span = k_ref.shape[1]
    first = lax.axis_index(SEQ) * span
    places = first + lanes((SUB, span))
    lane, sub = lanes((SUB, 128)), subs((SUB, 128))
    scale = 1.0 / math.sqrt(HEAD_DIM)
    for i in range(CHUNKS):
        scores = []
        for b in range(i * PER, (i + 1) * PER):
            query = qs[b * SUB : (b + 1) * SUB, :].astype(bf16)
            s = lax.dot_general(query, k_ref[b], (((1,), (1,)), ((), ())), preferred_element_type=f32)
            scores.append(jnp.where(places < lengths_ref[b], s * scale, masked_score))
        for n, b in enumerate(range(i * PER, (i + 1) * PER)):
            s = scores[n]
            peak = rounded(jnp.max(s, axis=-1, keepdims=True))
            p = jnp.where(places < lengths_ref[b], jnp.exp(s - peak), 0.0)
            total = jnp.sum(p, axis=-1, keepdims=True)
            p_hi = rounded(p)
            both = jnp.concatenate([p_hi, p - p_hi], axis=0).astype(bf16)
            weighted = jnp.dot(both, v_ref[b], preferred_element_type=f32)
            weighted = weighted[:SUB] + weighted[SUB:]
            stats = jnp.where(lane == sub, peak, 0.0)
            stats = jnp.where(lane == sub + SUB, total, stats)
            stats = jnp.sum(jnp.where(sub < GROUP, stats, 0.0), axis=0, keepdims=True)
            half, line = b // HALF, (b % HALF) * SUB
            halves[half, line : line + SUB, :] = jnp.where(sub == GROUP, stats, weighted)
    core = lax.axis_index("seq_2")
    keep_ref[...] = halves[core]
    send_ref[:HALF_ROWS, :] = halves[1 - core]


def as_column(x):
    shape = (HALF, SUB, 128)
    wide = jnp.broadcast_to(x, shape)
    return jnp.sum(jnp.where(lanes(shape) == subs(shape), wide, 0.0), axis=2, keepdims=True)


def merge_kernel(keep_ref, got_ref, weight_ref, ahead_ref, out_ref, packed):
    shape = (HALF, SUB, 128)
    sub = subs(shape)
    blocks = [ref[:HALF_ROWS, :].reshape(shape) for ref in (keep_ref, got_ref)]
    stats = [jnp.sum(jnp.where(sub == GROUP, x, 0.0), axis=1, keepdims=True) for x in blocks]
    peak = jnp.maximum(stats[0], stats[1])
    weighted, total = jnp.zeros(shape, f32), jnp.zeros((HALF, 1, 128), f32)
    for x, s in zip(blocks, stats):
        factor = jnp.exp(jnp.minimum(s - peak, 0.0))
        total += factor * pltpu.roll(s, 128 - SUB, 2)
        weighted += as_column(factor) * x
    flat = lanes((HALF, 1, 128))
    total_hi = rounded(total)
    line = jnp.where(flat < SUB, peak, pltpu.roll(total_hi, SUB, 2))
    line = jnp.where(flat < 2 * SUB, line, pltpu.roll(total - total_hi, 2 * SUB, 2))
    line = jnp.where(flat % SUB < GROUP, jnp.where(flat < 3 * SUB, line, 0.0), 0.0)
    tile, row, lane = jnp.zeros((SUB, 128), f32), subs((SUB, 128)), lanes((SUB, 128))
    for t in range(HALF):
        packed[GROUP * t : GROUP * (t + 1), :] = weighted[t, :GROUP, :]
        here = (row == t % SUB) & (lane // 32 == t // SUB)
        value = line[t] if t < SUB else pltpu.roll(line[t], 32, 1)
        tile = jnp.where(here, value, tile)
    packed[PACKED:, :] = tile
    block = packed[...].astype(bf16)
    for i in range(CHIPS):
        out_ref[i] = block


def others(ref, first, count):
    line = HALF_ROWS + first
    left = ref[line : line + count, :]
    return jnp.concatenate([left, ref[line + ROWS : line + ROWS + count, : COLS - 128]], axis=1)


def project_kernel(
    ids_ref, in_ref, hidden_ref, got_ref, weight_ref, other_ref, ahead_ref, out_ref, rest_ref, att, wide
):
    core, me = lax.axis_index("seq_2"), lax.axis_index("exp")
    tiles = [in_ref[i, PACKED:, :].astype(f32) for i in range(CHIPS)]
    peak = functools.reduce(jnp.maximum, tiles)
    factors = [jnp.exp(jnp.minimum(s - peak, 0.0)) for s in tiles]
    total = jnp.zeros((SUB, 128), f32)
    for s, factor in zip(tiles, factors):
        total += factor * (pltpu.roll(s, 128 - SUB, 1) + pltpu.roll(s, 128 - 2 * SUB, 1))
    lane = lanes((SUB, 128))
    inverse = 1.0 / jnp.where((lane % 32 < GROUP) & (total > 0.0), total, 1.0)
    row = lax.broadcasted_iota(jnp.int32, (PACKED, 2 * SUB), 0)
    column = lax.broadcasted_iota(jnp.int32, (PACKED, 2 * SUB), 1)
    spread = jnp.where((row // GROUP) % SUB == column % SUB, 1.0, 0.0).astype(bf16)
    row = subs((PACKED, 128))
    wanted = lanes((PACKED, 128)) == 32 * (row // GROUP // SUB) + row % GROUP
    weighted = jnp.zeros((PACKED, 128), f32)
    for i in range(CHIPS):
        factor = factors[i] * inverse
        factor_hi = rounded(factor)
        parts = jnp.concatenate([factor_hi, factor - factor_hi], axis=0).astype(bf16)
        wide_factor = jnp.dot(spread, parts, preferred_element_type=f32)
        factor = jnp.sum(jnp.where(wanted, wide_factor, 0.0), axis=-1, keepdims=True)
        weighted += factor * in_ref[i, :PACKED, :].astype(f32)
    att[:PACKED, :] = weighted
    acc, acc_other = jnp.zeros((HALF, COLS), f32), jnp.zeros((HALF, COLS), f32)
    over_features = (((1,), (1,)), ((), ()))
    for h in range(GROUP):
        rows = att[pl.ds(h, HALF, stride=GROUP), :].astype(bf16)
        cols = slice(h * HEAD_DIM, (h + 1) * HEAD_DIM)
        acc += lax.dot_general(rows, weight_ref[:, cols], over_features, preferred_element_type=f32)
        acc_other += lax.dot_general(rows, other_ref[:, cols], over_features, preferred_element_type=f32)
    mine = OWNED * me - HALF * core
    row = subs((HALF, COLS))
    hidden, hidden_other = hidden_ref[...].astype(f32), others(got_ref, 0, OWNED)
    for r in range(OWNED):
        acc += jnp.where(row == mine + r, hidden[r : r + 1, :], 0.0)
        acc_other += jnp.where(row == mine + r, hidden_other[r : r + 1, :], 0.0)
    row, lane = subs((ROWS, BOTH)), lanes((ROWS, BOTH))
    ids = jnp.zeros((ROWS, BOTH), f32)
    for r in range(OWNED):
        for k in range(2):
            here = (row == HALF) & (lane == 2 * (OWNED * me + r) + k)
            ids = jnp.where(here, ids_ref[k, r].astype(f32), ids)
    wide[...] = ids
    wide[:HALF, :COLS] = jnp.where(core == 0, acc, acc_other)
    wide[:HALF, COLS:] = jnp.where(core == 0, acc_other, acc)
    full = wide[...]
    sent = full.astype(bf16)
    for i in range(EXPERTS):
        out_ref[i] = sent
    owned = (row >= mine) & (row < mine + OWNED) & (row < HALF)
    rest_ref[...] = jnp.where(owned, full - sent.astype(f32), 0.0)


def gained_kernel(in_ref, rest_ref, gain_ref, router_ref, got_ref, ahead_ref, out_ref, residual_ref, wide):
    core = lax.axis_index("seq_2")
    total = rest_ref[...]
    for i in range(EXPERTS):
        total += in_ref[i].astype(f32)
    residual_ref[...] = total
    router, router_other = router_ref[...].astype(f32), others(got_ref, OWNED, EXPERTS)
    gain, gain_other = gain_ref[...], others(got_ref, OWNED + EXPERTS, 1)
    wide[:EXPERTS, :COLS] = jnp.where(core == 0, router, router_other)
    wide[:EXPERTS, COLS:] = jnp.where(core == 0, router_other, router)
    wide[EXPERTS : EXPERTS + 1, :COLS] = jnp.where(core == 0, gain, gain_other)
    wide[EXPERTS : EXPERTS + 1, COLS:] = jnp.where(core == 0, gain_other, gain)
    routers = wide[:EXPERTS, :].astype(bf16)
    row = subs((ROWS, BOTH))
    residual = jnp.where(row < HALF, total, 0.0)
    gained = residual * wide[EXPERTS : EXPERTS + 1, :]
    hi = gained.astype(bf16)
    lo = (gained - hi.astype(f32)).astype(bf16)
    over_features = (((1,), (1,)), ((), ()))
    logits = lax.dot_general(hi, routers, over_features, preferred_element_type=f32)
    logits += lax.dot_general(lo, routers, over_features, preferred_element_type=f32)
    squares = jnp.sum(residual * residual, axis=-1, keepdims=True)
    logits_hi, squares_hi = rounded(logits), rounded(squares)
    wide[:, :128] = jnp.zeros((ROWS, 128), f32)
    wide[:, :8] = logits_hi
    wide[:, 8:9] = squares_hi
    wide[:, 16:24] = logits - logits_hi
    wide[:, 24:25] = squares - squares_hi
    stats = wide[:, :128].astype(bf16)
    to = lax.broadcasted_iota(jnp.int32, (ROWS, ROWS), 0)
    source = lax.broadcasted_iota(jnp.int32, (ROWS, ROWS), 1)
    row = subs((ROWS, 128))
    for j in range(3):
        choice = jnp.where((to >= HALF) & (source == 3 * (to - HALF) + j), 1.0, 0.0).astype(bf16)
        packed = jnp.dot(choice, stats, preferred_element_type=f32)
        cols = slice(128 * j, 128 * (j + 1))
        sent = jnp.where(row < HALF, gained[:, cols], packed).astype(bf16)
        for i in range(CHIPS):
            out_ref[i, :, cols] = sent


def expert_kernel(
    capacity_ref, own_ref, other_ref, residual_ref, gate_ref, up_ref, down_ref, keep_ref, send_ref
):
    core, me = lax.axis_index("seq_2"), lax.axis_index("exp")
    sums = [jnp.zeros((ROWS, BOTH), f32) for _ in range(2)]
    gate = jnp.zeros((2 * ROWS, 256), f32)
    up = jnp.zeros((2 * ROWS, 256), f32)
    for k in range(CHIPS):
        own, other = own_ref[k], other_ref[k]
        pair = (jnp.where(core == 0, own, other), jnp.where(core == 0, other, own))
        for i in range(2):
            sums[i] += pair[i].astype(f32)
        x = jnp.concatenate(pair, axis=0)
        rows = slice(BOTH * k, BOTH * (k + 1))
        gate += jnp.dot(x, gate_ref[rows, :], preferred_element_type=f32)
        up += jnp.dot(x, up_ref[rows, :], preferred_element_type=f32)
    shape = (2 * ROWS, 128)
    lane, row = lanes(shape), subs(shape)
    stats = jnp.zeros(shape, f32)
    for half in range(2):
        for t in range(HALF):
            line = sums[half][HALF + t // 3 : HALF + t // 3 + 1, 128 * (t % 3) : 128 * (t % 3 + 1)]
            stats = jnp.where(row == ROWS * half + t, line, stats)
    stats += pltpu.roll(stats, 128 - 16, 1)

    def pick(x, place):
        return jnp.sum(jnp.where(lane == place, x, 0.0), axis=-1, keepdims=True)

    scale = lax.rsqrt(pick(stats, 8) / D + norm_eps)
    logits = stats * scale
    inside = row % ROWS
    token = HALF * (row // ROWS) + inside
    named = jnp.broadcast_to(residual_ref[HALF : HALF + 1, :128], shape)
    first, second = pick(named, 2 * token).astype(jnp.int32), pick(named, 2 * token + 1).astype(jnp.int32)
    names = (first == me) | (second == me)
    other = jnp.where(first == me, second, first)
    routed = 1.0 / (1.0 + jnp.exp(pick(logits, other) - pick(logits, me)))
    naming = jnp.broadcast_to(jnp.where(names, 1.0, 0.0), shape)
    place = inside % OWNED
    earlier = jnp.where(place >= 1, pltpu.roll(naming, 1, 0), 0.0)
    earlier += jnp.where(place >= 2, pltpu.roll(naming, 2, 0), 0.0)
    kept = names & (earlier[:, :1] < capacity_ref[me].astype(f32)) & (inside[:, :1] < HALF)
    weight = jnp.where(kept, routed, 0.0)
    gate, up = gate * scale, up * scale
    inner = (gate / (1.0 + jnp.exp(-gate)) * up * weight).astype(bf16)
    for k in range(CHIPS):
        y = jnp.dot(inner, down_ref[:, BOTH * k : BOTH * (k + 1)], preferred_element_type=f32)
        even, odd = y[:, :COLS], y[:, COLS:]
        keep_ref[k] = jnp.where(core == 0, even, odd)
        send_ref[k] = jnp.where(core == 0, odd, even).astype(bf16)
    residual = residual_ref[...]
    residual = jnp.where(core == 0, residual[:, COLS:], residual[:, :COLS])
    residual_hi = residual.astype(bf16)
    send_ref[CHIPS, :ROWS, :] = residual_hi
    send_ref[CHIPS, ROWS:, :] = (residual - residual_hi.astype(f32)).astype(bf16)


def pair_kernel(keep_ref, got_ref, out_ref):
    for k in range(CHIPS):
        total = keep_ref[k] + got_ref[k].astype(f32)
        for e in range(EXPERTS):
            line = ROWS * (e // 4) + OWNED * (e % 4)
            out_ref[EXPERTS * k + e, :, :COLS] = total[line : line + 2, :].astype(bf16)
            last = total[line + 2 : line + OWNED, :]
            last = jnp.concatenate([last[:, : COLS // 2], last[:, COLS // 2 :]], axis=0)
            out_ref[EXPERTS * k + e, :, COLS:] = last.astype(bf16)


def final_kernel(in_ref, residual_ref, got_ref, out_ref):
    core, me = lax.axis_index("seq_2"), lax.axis_index("exp")
    residual = residual_ref[...]
    own = jnp.where(core == 0, residual[:, :COLS], residual[:, COLS:])
    got = got_ref[CHIPS].astype(f32)
    residual = jnp.where(me // 4 == core, own, got[:ROWS] + got[ROWS:])
    total = jnp.zeros((OWNED, COLS), f32)
    for q in range(4):
        total += jnp.where(me % 4 == q, residual[OWNED * q : OWNED * (q + 1), :], 0.0)
    experts = jnp.sum(in_ref[...].astype(f32), axis=0)
    last = jnp.concatenate([experts[:1, COLS:], experts[1:, COLS:]], axis=1)
    out_ref[...] = (total + jnp.concatenate([experts[:, :COLS], last], axis=0)).astype(bf16)


def shaped(shape, dtype):
    return jax.ShapeDtypeStruct(shape, dtype)


def call(kernel, outs, specs, scratch=(), limit=6 << 20):
    single = not isinstance(outs, tuple)
    return pl.pallas_call(
        kernel,
        out_shape=outs,
        in_specs=list(specs),
        out_specs=VMEM if single else (VMEM,) * len(outs),
        scratch_shapes=list(scratch),
        compiler_params=pltpu.CompilerParams(vmem_limit_bytes=limit),
        cost_estimate=pl.CostEstimate(flops=1 << 20, bytes_accessed=1 << 20, transcendentals=0),
    )


def in_hbm(x):
    return pltpu.with_memory_space_constraint(x, pltpu.HBM)


def exchanged(value, axes):
    return lax.all_to_all(value, axes, 0, 0, tiled=True)


def swapped(value):
    return lax.ppermute(value, "seq_2", [(0, 1), (1, 0)])


def on_device(
    hidden_in,
    queries,
    key_cache,
    value_cache,
    lengths,
    out_weight,
    norm_gain,
    router,
    expert_ids,
    capacity,
    w_gate,
    w_up,
    w_down,
):
    keep, send = call(
        attention_kernel,
        (
            shaped((HALF_ROWS, 128), f32),
            shaped((HALF_ROWS + 2 * ROWS, 128), f32),
        ),
        (SMEM,) + (VMEM,) * 6,
        (
            pltpu.VMEM((TOKENS * SUB, 128), f32),
            pltpu.VMEM((2, HALF_ROWS, 128), f32),
        ),
        limit=8 << 20,
    )(*(in_hbm(x) for x in (lengths, queries, key_cache, value_cache, hidden_in, router.T, norm_gain[None, :])))
    weight = out_weight.T
    weight_other = swapped(weight)
    got_partial = swapped(send)
    partial = call(
        merge_kernel,
        shaped((CHIPS, BLOCK, 128), bf16),
        (VMEM,) * 4,
        (pltpu.VMEM((BLOCK, 128), f32),),
    )(keep, got_partial, weight_other, w_gate)
    partial = exchanged(partial, ("seq_0", "seq_1"))
    projected, rest = call(
        project_kernel,
        (shaped((EXPERTS, ROWS, BOTH), bf16), shaped((ROWS, BOTH), f32)),
        (SMEM,) + (VMEM,) * 6,
        (pltpu.VMEM((BLOCK, 128), f32), pltpu.VMEM((ROWS, BOTH), f32)),
    )(expert_ids.T, partial, hidden_in, got_partial, weight, weight_other, w_up)
    projected = exchanged(projected, "exp")
    gained, residual = call(
        gained_kernel,
        (shaped((CHIPS, ROWS, BOTH), bf16), shaped((ROWS, BOTH), f32)),
        (VMEM,) * 6,
        (pltpu.VMEM((ROWS, BOTH), f32),),
    )(projected, rest, norm_gain[None, :], router.T, got_partial, w_down)
    own = exchanged(gained, ("seq_0", "seq_1"))
    other = swapped(own)
    keep, send = call(
        expert_kernel,
        (shaped((CHIPS, 2 * ROWS, COLS), f32), shaped((CHIPS + 1, 2 * ROWS, COLS), bf16)),
        (SMEM,) + (VMEM,) * 6,
        limit=14 << 20,
    )(capacity, own, other, residual, w_gate[0], w_up[0], w_down[0])
    got = swapped(send)
    summed = call(pair_kernel, shaped((CHIPS * EXPERTS, 2, COLS + COLS // 2), bf16), (VMEM, VMEM))(keep, got)
    summed = exchanged(summed, ("seq_0", "seq_1", "exp"))
    return call(final_kernel, shaped((OWNED, COLS), bf16), (VMEM, VMEM, VMEM))(summed, residual, got)


def solution(mesh):
    split = Mesh(
        mesh.devices.reshape(4, 4, 2, mesh.shape["exp"]), ("seq_0", "seq_1", "seq_2", "exp")
    )
    placed = (
        P("exp", SEQ),
        P(None, "exp"),
        P(None, SEQ, "exp"),
        P(None, SEQ, "exp"),
        P(),
        P("exp", SEQ),
        P(SEQ),
        P(SEQ, None),
        P("exp", None),
        P(),
        P("exp", None, SEQ),
        P("exp", None, SEQ),
        P("exp", SEQ, None),
    )
    return jax.shard_map(
        on_device, mesh=split, in_specs=placed, out_specs=P("exp", SEQ), check_vma=False
    )
```

```python
import functools
import math

import jax
import jax.numpy as jnp
from jax import lax
from jax.experimental import pallas as pl
from jax.experimental.pallas import tpu as pltpu
from jax.sharding import Mesh
from jax.sharding import PartitionSpec as P

D = 6144
HEADS = 48
KV_HEADS = 8
HEAD_DIM = 128
EXPERTS = 8
TOKENS = 24
OWNED = 3
GROUP = HEADS // KV_HEADS
COLS = 192
HALF = TOKENS // 2
SUB = 8
HALF_ROWS = HALF * SUB
CHIPS = 16
SEQ = ("seq_0", "seq_1", "seq_2")
masked_score = -1e30
norm_eps = 1e-05
f32 = jnp.float32
bf16 = jnp.bfloat16
VMEM = pl.BlockSpec(memory_space=pltpu.VMEM)
SMEM = pl.BlockSpec(memory_space=pltpu.SMEM)


def lanes(shape):
    return lax.broadcasted_iota(jnp.int32, shape, len(shape) - 1)


def subs(shape):
    return lax.broadcasted_iota(jnp.int32, shape, len(shape) - 2)


def rounded(x):
    return x.astype(bf16).astype(f32)


CHUNKS = 4
PER = TOKENS // CHUNKS
BOTH = 2 * COLS
PACKED = HALF * GROUP
BLOCK = PACKED + SUB
ROWS = 16


def attention_kernel(
    lengths_ref, q_ref, k_ref, v_ref, hidden_ref, router_ref, gain_ref,
    keep_ref, send_ref, qs, halves,
):
    send_ref[HALF_ROWS:, :] = jnp.zeros((2 * ROWS, 128), f32)
    first = HALF_ROWS
    for ref in (hidden_ref, router_ref, gain_ref):
        lines = ref[...].astype(f32)
        send_ref[first : first + len(lines), :] = lines[:, :128]
        send_ref[first + ROWS : first + ROWS + len(lines), : COLS - 128] = lines[:, 128:]
        first += len(lines)
    qs[...] = jnp.zeros_like(qs)
    for h in range(GROUP):
        qs[pl.ds(h, TOKENS, stride=SUB), :] = q_ref[:, h * HEAD_DIM : (h + 1) * HEAD_DIM].astype(f32)
    span = k_ref.shape[1]
    first = lax.axis_index(SEQ) * span
    places = first + lanes((SUB, span))
    lane, sub = lanes((SUB, 128)), subs((SUB, 128))
    scale = 1.0 / math.sqrt(HEAD_DIM)
    for i in range(CHUNKS):
        scores = []
        for b in range(i * PER, (i + 1) * PER):
            query = qs[b * SUB : (b + 1) * SUB, :].astype(bf16)
            s = lax.dot_general(query, k_ref[b], (((1,), (1,)), ((), ())), preferred_element_type=f32)
            scores.append(jnp.where(places < lengths_ref[b], s * scale, masked_score))
        for n, b in enumerate(range(i * PER, (i + 1) * PER)):
            s = scores[n]
            peak = rounded(jnp.max(s, axis=-1, keepdims=True))
            p = jnp.where(places < lengths_ref[b], jnp.exp(s - peak), 0.0)
            total = jnp.sum(p, axis=-1, keepdims=True)
            p_hi = rounded(p)
            both = jnp.concatenate([p_hi, p - p_hi], axis=0).astype(bf16)
            weighted = jnp.dot(both, v_ref[b], preferred_element_type=f32)
            weighted = weighted[:SUB] + weighted[SUB:]
            stats = jnp.where(lane == sub, peak, 0.0)
            stats = jnp.where(lane == sub + SUB, total, stats)
            stats = jnp.sum(jnp.where(sub < GROUP, stats, 0.0), axis=0, keepdims=True)
            half, line = b // HALF, (b % HALF) * SUB
            halves[half, line : line + SUB, :] = jnp.where(sub == GROUP, stats, weighted)
    core = lax.axis_index("seq_2")
    keep_ref[...] = halves[core]
    send_ref[:HALF_ROWS, :] = halves[1 - core]


def as_column(x):
    shape = (HALF, SUB, 128)
    wide = jnp.broadcast_to(x, shape)
    return jnp.sum(jnp.where(lanes(shape) == subs(shape), wide, 0.0), axis=2, keepdims=True)


def merge_kernel(keep_ref, got_ref, weight_ref, ahead_ref, out_ref, packed):
    shape = (HALF, SUB, 128)
    sub = subs(shape)
    blocks = [ref[:HALF_ROWS, :].reshape(shape) for ref in (keep_ref, got_ref)]
    stats = [jnp.sum(jnp.where(sub == GROUP, x, 0.0), axis=1, keepdims=True) for x in blocks]
    peak = jnp.maximum(stats[0], stats[1])
    weighted, total = jnp.zeros(shape, f32), jnp.zeros((HALF, 1, 128), f32)
    for x, s in zip(blocks, stats):
        factor = jnp.exp(jnp.minimum(s - peak, 0.0))
        total += factor * pltpu.roll(s, 128 - SUB, 2)
        weighted += as_column(factor) * x
    flat = lanes((HALF, 1, 128))
    total_hi = rounded(total)
    line = jnp.where(flat < SUB, peak, pltpu.roll(total_hi, SUB, 2))
    line = jnp.where(flat < 2 * SUB, line, pltpu.roll(total - total_hi, 2 * SUB, 2))
    line = jnp.where(flat % SUB < GROUP, jnp.where(flat < 3 * SUB, line, 0.0), 0.0)
    tile, row, lane = jnp.zeros((SUB, 128), f32), subs((SUB, 128)), lanes((SUB, 128))
    for t in range(HALF):
        packed[GROUP * t : GROUP * (t + 1), :] = weighted[t, :GROUP, :]
        here = (row == t % SUB) & (lane // 32 == t // SUB)
        value = line[t] if t < SUB else pltpu.roll(line[t], 32, 1)
        tile = jnp.where(here, value, tile)
    packed[PACKED:, :] = tile
    block = packed[...].astype(bf16)
    for i in range(CHIPS):
        out_ref[i] = block


def others(ref, first, count):
    line = HALF_ROWS + first
    left = ref[line : line + count, :]
    return jnp.concatenate([left, ref[line + ROWS : line + ROWS + count, : COLS - 128]], axis=1)


def project_kernel(
    ids_ref, in_ref, hidden_ref, got_ref, weight_ref, other_ref, ahead_ref, out_ref, rest_ref, att, wide
):
    core, me = lax.axis_index("seq_2"), lax.axis_index("exp")
    tiles = [in_ref[i, PACKED:, :].astype(f32) for i in range(CHIPS)]
    peak = functools.reduce(jnp.maximum, tiles)
    factors = [jnp.exp(jnp.minimum(s - peak, 0.0)) for s in tiles]
    total = jnp.zeros((SUB, 128), f32)
    for s, factor in zip(tiles, factors):
        total += factor * (pltpu.roll(s, 128 - SUB, 1) + pltpu.roll(s, 128 - 2 * SUB, 1))
    lane = lanes((SUB, 128))
    inverse = 1.0 / jnp.where((lane % 32 < GROUP) & (total > 0.0), total, 1.0)
    row = lax.broadcasted_iota(jnp.int32, (PACKED, 2 * SUB), 0)
    column = lax.broadcasted_iota(jnp.int32, (PACKED, 2 * SUB), 1)
    spread = jnp.where((row // GROUP) % SUB == column % SUB, 1.0, 0.0).astype(bf16)
    row = subs((PACKED, 128))
    wanted = lanes((PACKED, 128)) == 32 * (row // GROUP // SUB) + row % GROUP
    weighted = jnp.zeros((PACKED, 128), f32)
    for i in range(CHIPS):
        factor = factors[i] * inverse
        factor_hi = rounded(factor)
        parts = jnp.concatenate([factor_hi, factor - factor_hi], axis=0).astype(bf16)
        wide_factor = jnp.dot(spread, parts, preferred_element_type=f32)
        factor = jnp.sum(jnp.where(wanted, wide_factor, 0.0), axis=-1, keepdims=True)
        weighted += factor * in_ref[i, :PACKED, :].astype(f32)
    att[:PACKED, :] = weighted
    acc, acc_other = jnp.zeros((HALF, COLS), f32), jnp.zeros((HALF, COLS), f32)
    over_features = (((1,), (1,)), ((), ()))
    for h in range(GROUP):
        rows = att[pl.ds(h, HALF, stride=GROUP), :].astype(bf16)
        cols = slice(h * HEAD_DIM, (h + 1) * HEAD_DIM)
        acc += lax.dot_general(rows, weight_ref[:, cols], over_features, preferred_element_type=f32)
        acc_other += lax.dot_general(rows, other_ref[:, cols], over_features, preferred_element_type=f32)
    mine = OWNED * me - HALF * core
    row = subs((HALF, COLS))
    hidden, hidden_other = hidden_ref[...].astype(f32), others(got_ref, 0, OWNED)
    for r in range(OWNED):
        acc += jnp.where(row == mine + r, hidden[r : r + 1, :], 0.0)
        acc_other += jnp.where(row == mine + r, hidden_other[r : r + 1, :], 0.0)
    row, lane = subs((ROWS, BOTH)), lanes((ROWS, BOTH))
    ids, given = jnp.zeros((ROWS, BOTH), f32), ids_ref[...].astype(f32)
    for r in range(OWNED):
        for k in range(2):
            here = (row == HALF) & (lane == 2 * (OWNED * me + r) + k)
            ids = jnp.where(here, given[k : k + 1, r : r + 1], ids)
    wide[...] = ids
    wide[:HALF, :COLS] = jnp.where(core == 0, acc, acc_other)
    wide[:HALF, COLS:] = jnp.where(core == 0, acc_other, acc)
    full = wide[...]
    sent = full.astype(bf16)
    for i in range(EXPERTS):
        out_ref[i] = sent
    owned = (row >= mine) & (row < mine + OWNED) & (row < HALF)
    rest_ref[...] = jnp.where(owned, full - sent.astype(f32), 0.0)


def gained_kernel(in_ref, rest_ref, gain_ref, router_ref, got_ref, ahead_ref, out_ref, residual_ref, wide):
    core = lax.axis_index("seq_2")
    total = rest_ref[...]
    for i in range(EXPERTS):
        total += in_ref[i].astype(f32)
    residual_ref[...] = total
    router, router_other = router_ref[...].astype(f32), others(got_ref, OWNED, EXPERTS)
    gain, gain_other = gain_ref[...], others(got_ref, OWNED + EXPERTS, 1)
    wide[:EXPERTS, :COLS] = jnp.where(core == 0, router, router_other)
    wide[:EXPERTS, COLS:] = jnp.where(core == 0, router_other, router)
    wide[EXPERTS : EXPERTS + 1, :COLS] = jnp.where(core == 0, gain, gain_other)
    wide[EXPERTS : EXPERTS + 1, COLS:] = jnp.where(core == 0, gain_other, gain)
    routers = wide[:EXPERTS, :].astype(bf16)
    row = subs((ROWS, BOTH))
    residual = jnp.where(row < HALF, total, 0.0)
    gained = residual * wide[EXPERTS : EXPERTS + 1, :]
    hi = gained.astype(bf16)
    lo = (gained - hi.astype(f32)).astype(bf16)
    over_features = (((1,), (1,)), ((), ()))
    logits = lax.dot_general(hi, routers, over_features, preferred_element_type=f32)
    logits += lax.dot_general(lo, routers, over_features, preferred_element_type=f32)
    squares = jnp.sum(residual * residual, axis=-1, keepdims=True)
    logits_hi, squares_hi = rounded(logits), rounded(squares)
    wide[:, :128] = jnp.zeros((ROWS, 128), f32)
    wide[:, :8] = logits_hi
    wide[:, 8:9] = squares_hi
    wide[:, 16:24] = logits - logits_hi
    wide[:, 24:25] = squares - squares_hi
    stats = wide[:, :128].astype(bf16)
    to = lax.broadcasted_iota(jnp.int32, (ROWS, ROWS), 0)
    source = lax.broadcasted_iota(jnp.int32, (ROWS, ROWS), 1)
    row = subs((ROWS, 128))
    for j in range(3):
        choice = jnp.where((to >= HALF) & (source == 3 * (to - HALF) + j), 1.0, 0.0).astype(bf16)
        packed = jnp.dot(choice, stats, preferred_element_type=f32)
        cols = slice(128 * j, 128 * (j + 1))
        sent = jnp.where(row < HALF, gained[:, cols], packed).astype(bf16)
        for i in range(CHIPS):
            out_ref[i, :, cols] = sent


def expert_kernel(
    capacity_ref, own_ref, other_ref, residual_ref, gate_ref, up_ref, down_ref, keep_ref, send_ref
):
    core, me = lax.axis_index("seq_2"), lax.axis_index("exp")
    sums = [jnp.zeros((ROWS, BOTH), f32) for _ in range(2)]
    gate = jnp.zeros((2 * ROWS, 256), f32)
    up = jnp.zeros((2 * ROWS, 256), f32)
    for k in range(CHIPS):
        own, other = own_ref[k], other_ref[k]
        pair = (jnp.where(core == 0, own, other), jnp.where(core == 0, other, own))
        for i in range(2):
            sums[i] += pair[i].astype(f32)
        x = jnp.concatenate(pair, axis=0)
        rows = slice(BOTH * k, BOTH * (k + 1))
        gate += jnp.dot(x, gate_ref[rows, :], preferred_element_type=f32)
        up += jnp.dot(x, up_ref[rows, :], preferred_element_type=f32)
    shape = (2 * ROWS, 128)
    lane, row = lanes(shape), subs(shape)
    stats = jnp.zeros(shape, f32)
    for half in range(2):
        for t in range(HALF):
            line = sums[half][HALF + t // 3 : HALF + t // 3 + 1, 128 * (t % 3) : 128 * (t % 3 + 1)]
            stats = jnp.where(row == ROWS * half + t, line, stats)
    stats += pltpu.roll(stats, 128 - 16, 1)

    def pick(x, place):
        return jnp.sum(jnp.where(lane == place, x, 0.0), axis=-1, keepdims=True)

    scale = lax.rsqrt(pick(stats, 8) / D + norm_eps)
    logits = stats * scale
    inside = row % ROWS
    token = HALF * (row // ROWS) + inside
    named = jnp.broadcast_to(residual_ref[HALF : HALF + 1, :128], shape)
    first, second = pick(named, 2 * token).astype(jnp.int32), pick(named, 2 * token + 1).astype(jnp.int32)
    names = (first == me) | (second == me)
    other = jnp.where(first == me, second, first)
    routed = 1.0 / (1.0 + jnp.exp(pick(logits, other) - pick(logits, me)))
    naming = jnp.broadcast_to(jnp.where(names, 1.0, 0.0), shape)
    place = inside % OWNED
    earlier = jnp.where(place >= 1, pltpu.roll(naming, 1, 0), 0.0)
    earlier += jnp.where(place >= 2, pltpu.roll(naming, 2, 0), 0.0)
    limits = capacity_ref[...].astype(f32)
    limit = jnp.sum(jnp.where(lanes((1, EXPERTS)) == me, limits, 0.0), axis=-1, keepdims=True)
    kept = names & (earlier[:, :1] < limit) & (inside[:, :1] < HALF)
    weight = jnp.where(kept, routed, 0.0)
    gate, up = gate * scale, up * scale
    inner = (gate / (1.0 + jnp.exp(-gate)) * up * weight).astype(bf16)
    for k in range(CHIPS):
        y = jnp.dot(inner, down_ref[:, BOTH * k : BOTH * (k + 1)], preferred_element_type=f32)
        even, odd = y[:, :COLS], y[:, COLS:]
        keep_ref[k] = jnp.where(core == 0, even, odd)
        send_ref[k] = jnp.where(core == 0, odd, even).astype(bf16)
    residual = residual_ref[...]
    residual = jnp.where(core == 0, residual[:, COLS:], residual[:, :COLS])
    residual_hi = residual.astype(bf16)
    send_ref[CHIPS, :ROWS, :] = residual_hi
    send_ref[CHIPS, ROWS:, :] = (residual - residual_hi.astype(f32)).astype(bf16)


def pair_kernel(keep_ref, got_ref, out_ref):
    first = subs((2 * ROWS, COLS // 2)) % ROWS % OWNED == 0
    for k in range(CHIPS):
        total = keep_ref[k] + got_ref[k].astype(f32)
        left, right = total[:, : COLS // 2], total[:, COLS // 2 :]
        left = jnp.concatenate([left[2:], left[:2]], axis=0)
        right = jnp.concatenate([right[1:], right[:1]], axis=0)
        wide = jnp.concatenate([total, jnp.where(first, left, right)], axis=1)
        for e in range(EXPERTS):
            line = ROWS * (e // 4) + OWNED * (e % 4)
            out_ref[EXPERTS * k + e] = wide[line : line + 2, :].astype(bf16)


def final_kernel(in_ref, residual_ref, got_ref, out_ref):
    core, me = lax.axis_index("seq_2"), lax.axis_index("exp")
    residual = residual_ref[...]
    own = jnp.where(core == 0, residual[:, :COLS], residual[:, COLS:])
    got = got_ref[CHIPS].astype(f32)
    residual = jnp.where(me // 4 == core, own, got[:ROWS] + got[ROWS:])
    total = jnp.zeros((OWNED, COLS), f32)
    for q in range(4):
        total += jnp.where(me % 4 == q, residual[OWNED * q : OWNED * (q + 1), :], 0.0)
    experts = jnp.sum(in_ref[...].astype(f32), axis=0)
    last = jnp.concatenate([experts[:1, COLS:], experts[1:, COLS:]], axis=1)
    out_ref[...] = (total + jnp.concatenate([experts[:, :COLS], last], axis=0)).astype(bf16)


def shaped(shape, dtype):
    return jax.ShapeDtypeStruct(shape, dtype)


def call(kernel, outs, specs, scratch=(), limit=6 << 20):
    single = not isinstance(outs, tuple)
    return pl.pallas_call(
        kernel,
        out_shape=outs,
        in_specs=list(specs),
        out_specs=VMEM if single else (VMEM,) * len(outs),
        scratch_shapes=list(scratch),
        compiler_params=pltpu.CompilerParams(vmem_limit_bytes=limit),
        cost_estimate=pl.CostEstimate(flops=1 << 20, bytes_accessed=1 << 20, transcendentals=0),
    )


def in_hbm(x):
    return pltpu.with_memory_space_constraint(x, pltpu.HBM)


def exchanged(value, axes):
    return lax.all_to_all(value, axes, 0, 0, tiled=True)


def swapped(value):
    return lax.ppermute(value, "seq_2", [(0, 1), (1, 0)])


def on_device(
    hidden_in,
    queries,
    key_cache,
    value_cache,
    lengths,
    out_weight,
    norm_gain,
    router,
    expert_ids,
    capacity,
    w_gate,
    w_up,
    w_down,
):
    keep, send = call(
        attention_kernel,
        (
            shaped((HALF_ROWS, 128), f32),
            shaped((HALF_ROWS + 2 * ROWS, 128), f32),
        ),
        (SMEM,) + (VMEM,) * 6,
        (
            pltpu.VMEM((TOKENS * SUB, 128), f32),
            pltpu.VMEM((2, HALF_ROWS, 128), f32),
        ),
        limit=8 << 20,
    )(*(in_hbm(x) for x in (lengths, queries, key_cache, value_cache, hidden_in, router.T, norm_gain[None, :])))
    weight = out_weight.T
    weight_other = swapped(weight)
    got_partial = swapped(send)
    partial = call(
        merge_kernel,
        shaped((CHIPS, BLOCK, 128), bf16),
        (VMEM,) * 4,
        (pltpu.VMEM((BLOCK, 128), f32),),
    )(keep, got_partial, weight_other, w_gate)
    partial = exchanged(partial, ("seq_0", "seq_1"))
    projected, rest = call(
        project_kernel,
        (shaped((EXPERTS, ROWS, BOTH), bf16), shaped((ROWS, BOTH), f32)),
        (VMEM,) * 7,
        (pltpu.VMEM((BLOCK, 128), f32), pltpu.VMEM((ROWS, BOTH), f32)),
    )(expert_ids.T, partial, hidden_in, got_partial, weight, weight_other, w_up)
    projected = exchanged(projected, "exp")
    gained, residual = call(
        gained_kernel,
        (shaped((CHIPS, ROWS, BOTH), bf16), shaped((ROWS, BOTH), f32)),
        (VMEM,) * 6,
        (pltpu.VMEM((ROWS, BOTH), f32),),
    )(projected, rest, norm_gain[None, :], router.T, got_partial, w_down)
    own = exchanged(gained, ("seq_0", "seq_1"))
    other = swapped(own)
    keep, send = call(
        expert_kernel,
        (shaped((CHIPS, 2 * ROWS, COLS), f32), shaped((CHIPS + 1, 2 * ROWS, COLS), bf16)),
        (VMEM,) * 7,
        limit=14 << 20,
    )(capacity[None, :], own, other, residual, w_gate[0], w_up[0], w_down[0])
    got = swapped(send)
    summed = call(pair_kernel, shaped((CHIPS * EXPERTS, 2, COLS + COLS // 2), bf16), (VMEM, VMEM))(keep, got)
    summed = exchanged(summed, ("seq_0", "seq_1", "exp"))
    return call(final_kernel, shaped((OWNED, COLS), bf16), (VMEM, VMEM, VMEM))(summed, residual, got)


def solution(mesh):
    split = Mesh(
        mesh.devices.reshape(4, 4, 2, mesh.shape["exp"]), ("seq_0", "seq_1", "seq_2", "exp")
    )
    placed = (
        P("exp", SEQ),
        P(None, "exp"),
        P(None, SEQ, "exp"),
        P(None, SEQ, "exp"),
        P(),
        P("exp", SEQ),
        P(SEQ),
        P(SEQ, None),
        P("exp", None),
        P(),
        P("exp", None, SEQ),
        P("exp", None, SEQ),
        P("exp", SEQ, None),
    )
    return jax.shard_map(
        on_device, mesh=split, in_specs=placed, out_specs=P("exp", SEQ), check_vma=False
    )
```

```python
import functools
import math

import jax
import jax.numpy as jnp
from jax import lax
from jax.experimental import pallas as pl
from jax.experimental.pallas import tpu as pltpu
from jax.sharding import Mesh
from jax.sharding import PartitionSpec as P

D = 6144
HEADS = 48
KV_HEADS = 8
HEAD_DIM = 128
EXPERTS = 8
TOKENS = 24
OWNED = 3
GROUP = HEADS // KV_HEADS
COLS = 192
HALF = TOKENS // 2
SUB = 8
HALF_ROWS = HALF * SUB
CHIPS = 16
SEQ = ("seq_0", "seq_1", "seq_2")
masked_score = -1e30
norm_eps = 1e-05
f32 = jnp.float32
bf16 = jnp.bfloat16
VMEM = pl.BlockSpec(memory_space=pltpu.VMEM)
SMEM = pl.BlockSpec(memory_space=pltpu.SMEM)


def lanes(shape):
    return lax.broadcasted_iota(jnp.int32, shape, len(shape) - 1)


def subs(shape):
    return lax.broadcasted_iota(jnp.int32, shape, len(shape) - 2)


def rounded(x):
    return x.astype(bf16).astype(f32)


CHUNKS = 4
PER = TOKENS // CHUNKS
BOTH = 2 * COLS
PACKED = HALF * GROUP
BLOCK = PACKED + SUB
ROWS = 16


def attention_kernel(
    lengths_ref, q_ref, k_ref, v_ref, hidden_ref, router_ref, gain_ref,
    keep_ref, send_ref, qs, halves,
):
    send_ref[HALF_ROWS:, :] = jnp.zeros((2 * ROWS, 128), f32)
    first = HALF_ROWS
    for ref in (hidden_ref, router_ref, gain_ref):
        lines = ref[...].astype(f32)
        send_ref[first : first + len(lines), :] = lines[:, :128]
        send_ref[first + ROWS : first + ROWS + len(lines), : COLS - 128] = lines[:, 128:]
        first += len(lines)
    qs[...] = jnp.zeros_like(qs)
    for h in range(GROUP):
        qs[pl.ds(h, TOKENS, stride=SUB), :] = q_ref[:, h * HEAD_DIM : (h + 1) * HEAD_DIM].astype(f32)
    span = k_ref.shape[1]
    first = lax.axis_index(SEQ) * span
    places = first + lanes((SUB, span))
    lane, sub = lanes((SUB, 128)), subs((SUB, 128))
    scale = 1.0 / math.sqrt(HEAD_DIM)
    for i in range(CHUNKS):
        scores = []
        for b in range(i * PER, (i + 1) * PER):
            query = qs[b * SUB : (b + 1) * SUB, :].astype(bf16)
            s = lax.dot_general(query, k_ref[b], (((1,), (1,)), ((), ())), preferred_element_type=f32)
            scores.append(jnp.where(places < lengths_ref[b], s * scale, masked_score))
        for n, b in enumerate(range(i * PER, (i + 1) * PER)):
            s = scores[n]
            peak = rounded(jnp.max(s, axis=-1, keepdims=True))
            p = jnp.where(places < lengths_ref[b], jnp.exp(s - peak), 0.0)
            total = jnp.sum(p, axis=-1, keepdims=True)
            p_hi = rounded(p)
            both = jnp.concatenate([p_hi, p - p_hi], axis=0).astype(bf16)
            weighted = jnp.dot(both, v_ref[b], preferred_element_type=f32)
            weighted = weighted[:SUB] + weighted[SUB:]
            stats = jnp.where(lane == sub, peak, 0.0)
            stats = jnp.where(lane == sub + SUB, total, stats)
            stats = jnp.sum(jnp.where(sub < GROUP, stats, 0.0), axis=0, keepdims=True)
            half, line = b // HALF, (b % HALF) * SUB
            halves[half, line : line + SUB, :] = jnp.where(sub == GROUP, stats, weighted)
    core = lax.axis_index("seq_2")
    keep_ref[...] = halves[core]
    send_ref[:HALF_ROWS, :] = halves[1 - core]


def as_column(x):
    shape = (HALF, SUB, 128)
    wide = jnp.broadcast_to(x, shape)
    return jnp.sum(jnp.where(lanes(shape) == subs(shape), wide, 0.0), axis=2, keepdims=True)


def merge_kernel(keep_ref, got_ref, weight_ref, ahead_ref, out_ref, packed):
    shape = (HALF, SUB, 128)
    sub = subs(shape)
    blocks = [ref[:HALF_ROWS, :].reshape(shape) for ref in (keep_ref, got_ref)]
    stats = [jnp.sum(jnp.where(sub == GROUP, x, 0.0), axis=1, keepdims=True) for x in blocks]
    peak = jnp.maximum(stats[0], stats[1])
    weighted, total = jnp.zeros(shape, f32), jnp.zeros((HALF, 1, 128), f32)
    for x, s in zip(blocks, stats):
        factor = jnp.exp(jnp.minimum(s - peak, 0.0))
        total += factor * pltpu.roll(s, 128 - SUB, 2)
        weighted += as_column(factor) * x
    flat = lanes((HALF, 1, 128))
    total_hi = rounded(total)
    line = jnp.where(flat < SUB, peak, pltpu.roll(total_hi, SUB, 2))
    line = jnp.where(flat < 2 * SUB, line, pltpu.roll(total - total_hi, 2 * SUB, 2))
    line = jnp.where(flat % SUB < GROUP, jnp.where(flat < 3 * SUB, line, 0.0), 0.0)
    tile, row, lane = jnp.zeros((SUB, 128), f32), subs((SUB, 128)), lanes((SUB, 128))
    for t in range(HALF):
        packed[GROUP * t : GROUP * (t + 1), :] = weighted[t, :GROUP, :]
        here = (row == t % SUB) & (lane // 32 == t // SUB)
        value = line[t] if t < SUB else pltpu.roll(line[t], 32, 1)
        tile = jnp.where(here, value, tile)
    packed[PACKED:, :] = tile
    block = packed[...].astype(bf16)
    for i in range(CHIPS):
        out_ref[i] = block


def others(ref, first, count):
    line = HALF_ROWS + first
    left = ref[line : line + count, :]
    return jnp.concatenate([left, ref[line + ROWS : line + ROWS + count, : COLS - 128]], axis=1)


def project_kernel(
    ids_ref, in_ref, hidden_ref, got_ref, weight_ref, other_ref, ahead_ref, out_ref, rest_ref, att, wide
):
    core, me = lax.axis_index("seq_2"), lax.axis_index("exp")
    tiles = [in_ref[i, PACKED:, :].astype(f32) for i in range(CHIPS)]
    peak = functools.reduce(jnp.maximum, tiles)
    factors = [jnp.exp(jnp.minimum(s - peak, 0.0)) for s in tiles]
    total = jnp.zeros((SUB, 128), f32)
    for s, factor in zip(tiles, factors):
        total += factor * (pltpu.roll(s, 128 - SUB, 1) + pltpu.roll(s, 128 - 2 * SUB, 1))
    lane = lanes((SUB, 128))
    inverse = 1.0 / jnp.where((lane % 32 < GROUP) & (total > 0.0), total, 1.0)
    row = lax.broadcasted_iota(jnp.int32, (PACKED, 2 * SUB), 0)
    column = lax.broadcasted_iota(jnp.int32, (PACKED, 2 * SUB), 1)
    spread = jnp.where((row // GROUP) % SUB == column % SUB, 1.0, 0.0).astype(bf16)
    row = subs((PACKED, 128))
    wanted = lanes((PACKED, 128)) == 32 * (row // GROUP // SUB) + row % GROUP
    weighted = jnp.zeros((PACKED, 128), f32)
    for i in range(CHIPS):
        factor = factors[i] * inverse
        factor_hi = rounded(factor)
        parts = jnp.concatenate([factor_hi, factor - factor_hi], axis=0).astype(bf16)
        wide_factor = jnp.dot(spread, parts, preferred_element_type=f32)
        factor = jnp.sum(jnp.where(wanted, wide_factor, 0.0), axis=-1, keepdims=True)
        weighted += factor * in_ref[i, :PACKED, :].astype(f32)
    att[:PACKED, :] = weighted
    acc, acc_other = jnp.zeros((HALF, COLS), f32), jnp.zeros((HALF, COLS), f32)
    over_features = (((1,), (1,)), ((), ()))
    for h in range(GROUP):
        rows = att[pl.ds(h, HALF, stride=GROUP), :].astype(bf16)
        cols = slice(h * HEAD_DIM, (h + 1) * HEAD_DIM)
        acc += lax.dot_general(rows, weight_ref[:, cols], over_features, preferred_element_type=f32)
        acc_other += lax.dot_general(rows, other_ref[:, cols], over_features, preferred_element_type=f32)
    mine = OWNED * me - HALF * core
    row = subs((HALF, COLS))
    hidden, hidden_other = hidden_ref[...].astype(f32), others(got_ref, 0, OWNED)
    for r in range(OWNED):
        acc += jnp.where(row == mine + r, hidden[r : r + 1, :], 0.0)
        acc_other += jnp.where(row == mine + r, hidden_other[r : r + 1, :], 0.0)
    row, lane = subs((ROWS, BOTH)), lanes((ROWS, BOTH))
    ids, given = jnp.zeros((ROWS, BOTH), f32), ids_ref[...].astype(f32)
    for r in range(OWNED):
        for k in range(2):
            here = (row == HALF) & (lane == 2 * (OWNED * me + r) + k)
            ids = jnp.where(here, given[k : k + 1, r : r + 1], ids)
    wide[...] = ids
    wide[:HALF, :COLS] = jnp.where(core == 0, acc, acc_other)
    wide[:HALF, COLS:] = jnp.where(core == 0, acc_other, acc)
    full = wide[...]
    sent = full.astype(bf16)
    for i in range(EXPERTS):
        out_ref[i] = sent
    owned = (row >= mine) & (row < mine + OWNED) & (row < HALF)
    rest_ref[...] = jnp.where(owned, full - sent.astype(f32), 0.0)


def gained_kernel(in_ref, rest_ref, gain_ref, router_ref, got_ref, ahead_ref, out_ref, residual_ref, wide):
    core = lax.axis_index("seq_2")
    total = rest_ref[...]
    for i in range(EXPERTS):
        total += in_ref[i].astype(f32)
    residual_ref[...] = total
    router, router_other = router_ref[...].astype(f32), others(got_ref, OWNED, EXPERTS)
    gain, gain_other = gain_ref[...], others(got_ref, OWNED + EXPERTS, 1)
    wide[:EXPERTS, :COLS] = jnp.where(core == 0, router, router_other)
    wide[:EXPERTS, COLS:] = jnp.where(core == 0, router_other, router)
    wide[EXPERTS : EXPERTS + 1, :COLS] = jnp.where(core == 0, gain, gain_other)
    wide[EXPERTS : EXPERTS + 1, COLS:] = jnp.where(core == 0, gain_other, gain)
    routers = wide[:EXPERTS, :].astype(bf16)
    row = subs((ROWS, BOTH))
    residual = jnp.where(row < HALF, total, 0.0)
    gained = residual * wide[EXPERTS : EXPERTS + 1, :]
    hi = gained.astype(bf16)
    lo = (gained - hi.astype(f32)).astype(bf16)
    over_features = (((1,), (1,)), ((), ()))
    logits = lax.dot_general(hi, routers, over_features, preferred_element_type=f32)
    logits += lax.dot_general(lo, routers, over_features, preferred_element_type=f32)
    squares = jnp.sum(residual * residual, axis=-1, keepdims=True)
    logits_hi, squares_hi = rounded(logits), rounded(squares)
    wide[:, :128] = jnp.zeros((ROWS, 128), f32)
    wide[:, :8] = logits_hi
    wide[:, 8:9] = squares_hi
    wide[:, 16:24] = logits - logits_hi
    wide[:, 24:25] = squares - squares_hi
    stats = wide[:, :128].astype(bf16)
    to = lax.broadcasted_iota(jnp.int32, (ROWS, ROWS), 0)
    source = lax.broadcasted_iota(jnp.int32, (ROWS, ROWS), 1)
    row = subs((ROWS, 128))
    for j in range(3):
        choice = jnp.where((to >= HALF) & (source == 3 * (to - HALF) + j), 1.0, 0.0).astype(bf16)
        packed = jnp.dot(choice, stats, preferred_element_type=f32)
        cols = slice(128 * j, 128 * (j + 1))
        sent = jnp.where(row < HALF, gained[:, cols], packed).astype(bf16)
        for i in range(CHIPS):
            out_ref[i, :, cols] = sent


def expert_kernel(
    capacity_ref, own_ref, other_ref, residual_ref, gate_ref, up_ref, down_ref, keep_ref, send_ref
):
    core, me = lax.axis_index("seq_2"), lax.axis_index("exp")
    sums = [jnp.zeros((ROWS, BOTH), f32) for _ in range(2)]
    gate = jnp.zeros((2 * ROWS, 256), f32)
    up = jnp.zeros((2 * ROWS, 256), f32)
    for k in range(CHIPS):
        own, other = own_ref[k], other_ref[k]
        pair = (jnp.where(core == 0, own, other), jnp.where(core == 0, other, own))
        for i in range(2):
            sums[i] += pair[i].astype(f32)
        x = jnp.concatenate(pair, axis=0)
        rows = slice(BOTH * k, BOTH * (k + 1))
        gate += jnp.dot(x, gate_ref[rows, :], preferred_element_type=f32)
        up += jnp.dot(x, up_ref[rows, :], preferred_element_type=f32)
    shape = (2 * ROWS, 128)
    lane, row = lanes(shape), subs(shape)
    stats = jnp.zeros(shape, f32)
    for half in range(2):
        for t in range(HALF):
            line = sums[half][HALF + t // 3 : HALF + t // 3 + 1, 128 * (t % 3) : 128 * (t % 3 + 1)]
            stats = jnp.where(row == ROWS * half + t, line, stats)
    stats += pltpu.roll(stats, 128 - 16, 1)

    def pick(x, place):
        return jnp.sum(jnp.where(lane == place, x, 0.0), axis=-1, keepdims=True)

    scale = lax.rsqrt(pick(stats, 8) / D + norm_eps)
    logits = stats * scale
    inside = row % ROWS
    token = HALF * (row // ROWS) + inside
    named = jnp.broadcast_to(residual_ref[HALF : HALF + 1, :128], shape)
    first, second = pick(named, 2 * token).astype(jnp.int32), pick(named, 2 * token + 1).astype(jnp.int32)
    names = (first == me) | (second == me)
    other = jnp.where(first == me, second, first)
    routed = 1.0 / (1.0 + jnp.exp(pick(logits, other) - pick(logits, me)))
    naming = jnp.broadcast_to(jnp.where(names, 1.0, 0.0), shape)
    place = inside % OWNED
    earlier = jnp.where(place >= 1, pltpu.roll(naming, 1, 0), 0.0)
    earlier += jnp.where(place >= 2, pltpu.roll(naming, 2, 0), 0.0)
    limits = capacity_ref[...].astype(f32)
    limit = jnp.sum(jnp.where(lanes((1, EXPERTS)) == me, limits, 0.0), axis=-1, keepdims=True)
    kept = names & (earlier[:, :1] < limit) & (inside[:, :1] < HALF)
    weight = jnp.where(kept, routed, 0.0)
    gate, up = gate * scale, up * scale
    inner = (gate / (1.0 + jnp.exp(-gate)) * up * weight).astype(bf16)
    for k in range(CHIPS):
        y = jnp.dot(inner, down_ref[:, BOTH * k : BOTH * (k + 1)], preferred_element_type=f32)
        even, odd = y[:, :COLS], y[:, COLS:]
        keep_ref[k] = jnp.where(core == 0, even, odd)
        send_ref[k] = jnp.where(core == 0, odd, even).astype(bf16)
    residual = residual_ref[...]
    residual = jnp.where(core == 0, residual[:, COLS:], residual[:, :COLS])
    residual_hi = residual.astype(bf16)
    send_ref[CHIPS, :ROWS, :] = residual_hi
    send_ref[CHIPS, ROWS:, :] = (residual - residual_hi.astype(f32)).astype(bf16)


def pair_kernel(keep_ref, got_ref, out_ref):
    first = subs((2 * ROWS, COLS // 2)) % ROWS % OWNED == 0
    for k in range(CHIPS):
        total = keep_ref[k] + got_ref[k].astype(f32)
        left, right = total[:, : COLS // 2], total[:, COLS // 2 :]
        left = jnp.concatenate([left[2:], left[:2]], axis=0)
        right = jnp.concatenate([right[1:], right[:1]], axis=0)
        wide = jnp.concatenate([total, jnp.where(first, left, right)], axis=1)
        for e in range(EXPERTS):
            line = ROWS * (e // 4) + OWNED * (e % 4)
            out_ref[EXPERTS * k + e] = wide[line : line + 2, :].astype(bf16)


def final_kernel(in_ref, residual_ref, got_ref, out_ref):
    core, me = lax.axis_index("seq_2"), lax.axis_index("exp")
    residual = residual_ref[...]
    own = jnp.where(core == 0, residual[:, :COLS], residual[:, COLS:])
    got = got_ref[CHIPS].astype(f32)
    residual = jnp.where(me // 4 == core, own, got[:ROWS] + got[ROWS:])
    total = jnp.zeros((OWNED, COLS), f32)
    for q in range(4):
        total += jnp.where(me % 4 == q, residual[OWNED * q : OWNED * (q + 1), :], 0.0)
    parts = [jnp.sum(in_ref[CHIPS * i : CHIPS * (i + 1)].astype(f32), axis=0) for i in range(EXPERTS)]
    while len(parts) > 1:
        parts = [x + y for x, y in zip(parts[::2], parts[1::2])]
    experts = parts[0]
    last = jnp.concatenate([experts[:1, COLS:], experts[1:, COLS:]], axis=1)
    out_ref[...] = (total + jnp.concatenate([experts[:, :COLS], last], axis=0)).astype(bf16)


def shaped(shape, dtype):
    return jax.ShapeDtypeStruct(shape, dtype)


def call(kernel, outs, specs, scratch=(), limit=6 << 20):
    single = not isinstance(outs, tuple)
    return pl.pallas_call(
        kernel,
        out_shape=outs,
        in_specs=list(specs),
        out_specs=VMEM if single else (VMEM,) * len(outs),
        scratch_shapes=list(scratch),
        compiler_params=pltpu.CompilerParams(vmem_limit_bytes=limit),
        cost_estimate=pl.CostEstimate(flops=1 << 20, bytes_accessed=1 << 20, transcendentals=0),
    )


def in_hbm(x):
    return pltpu.with_memory_space_constraint(x, pltpu.HBM)


def exchanged(value, axes):
    return lax.all_to_all(value, axes, 0, 0, tiled=True)


def swapped(value):
    return lax.ppermute(value, "seq_2", [(0, 1), (1, 0)])


def on_device(
    hidden_in,
    queries,
    key_cache,
    value_cache,
    lengths,
    out_weight,
    norm_gain,
    router,
    expert_ids,
    capacity,
    w_gate,
    w_up,
    w_down,
):
    keep, send = call(
        attention_kernel,
        (
            shaped((HALF_ROWS, 128), f32),
            shaped((HALF_ROWS + 2 * ROWS, 128), f32),
        ),
        (SMEM,) + (VMEM,) * 6,
        (
            pltpu.VMEM((TOKENS * SUB, 128), f32),
            pltpu.VMEM((2, HALF_ROWS, 128), f32),
        ),
        limit=8 << 20,
    )(*(in_hbm(x) for x in (lengths, queries, key_cache, value_cache, hidden_in, router.T, norm_gain[None, :])))
    weight = out_weight.T
    weight_other = swapped(weight)
    got_partial = swapped(send)
    partial = call(
        merge_kernel,
        shaped((CHIPS, BLOCK, 128), bf16),
        (VMEM,) * 4,
        (pltpu.VMEM((BLOCK, 128), f32),),
    )(keep, got_partial, weight_other, w_gate)
    partial = exchanged(partial, ("seq_0", "seq_1"))
    projected, rest = call(
        project_kernel,
        (shaped((EXPERTS, ROWS, BOTH), bf16), shaped((ROWS, BOTH), f32)),
        (VMEM,) * 7,
        (pltpu.VMEM((BLOCK, 128), f32), pltpu.VMEM((ROWS, BOTH), f32)),
    )(expert_ids.T, partial, hidden_in, got_partial, weight, weight_other, w_up)
    projected = exchanged(projected, "exp")
    gained, residual = call(
        gained_kernel,
        (shaped((CHIPS, ROWS, BOTH), bf16), shaped((ROWS, BOTH), f32)),
        (VMEM,) * 6,
        (pltpu.VMEM((ROWS, BOTH), f32),),
    )(projected, rest, norm_gain[None, :], router.T, got_partial, w_down)
    own = exchanged(gained, ("seq_0", "seq_1"))
    other = swapped(own)
    keep, send = call(
        expert_kernel,
        (shaped((CHIPS, 2 * ROWS, COLS), f32), shaped((CHIPS + 1, 2 * ROWS, COLS), bf16)),
        (VMEM,) * 7,
        limit=14 << 20,
    )(capacity[None, :], own, other, residual, w_gate[0], w_up[0], w_down[0])
    got = swapped(send)
    summed = call(pair_kernel, shaped((CHIPS * EXPERTS, 2, COLS + COLS // 2), bf16), (VMEM, VMEM))(keep, got)
    summed = exchanged(summed, ("seq_0", "seq_1", "exp"))
    return call(final_kernel, shaped((OWNED, COLS), bf16), (VMEM, VMEM, VMEM))(summed, residual, got)


def solution(mesh):
    split = Mesh(
        mesh.devices.reshape(4, 4, 2, mesh.shape["exp"]), ("seq_0", "seq_1", "seq_2", "exp")
    )
    placed = (
        P("exp", SEQ),
        P(None, "exp"),
        P(None, SEQ, "exp"),
        P(None, SEQ, "exp"),
        P(),
        P("exp", SEQ),
        P(SEQ),
        P(SEQ, None),
        P("exp", None),
        P(),
        P("exp", None, SEQ),
        P("exp", None, SEQ),
        P("exp", SEQ, None),
    )
    return jax.shard_map(
        on_device, mesh=split, in_specs=placed, out_specs=P("exp", SEQ), check_vma=False
    )
```
